32 devices in a mesh: row: 4 (over x, core), col: 8 (over z, y).
Axes of the slice: x: 2, y: 2, z: 4, core: 2. Of those that a mesh axis runs over, the one named last changes fastest.
Arguments:
- prior: float32 [16384, 16384], P('row', 'col'), may hold values from -6 to 6
- ozone_courant: float32 [16384], replicated, may hold values from 0.05 to 0.5
- ozone_diffusion: float32 [16384], replicated, may hold values from 0.02 to 0.25
- ozone_wind: int32 [16384], replicated, may hold values from 0 to 1
- carbon_courant: float32 [16384], replicated, may hold values from 0.05 to 0.5
- carbon_diffusion: float32 [16384], replicated, may hold values from 0.02 to 0.25
- carbon_wind: int32 [16384], replicated, may hold values from 0 to 1
- ozone_sites: int32 [2, 512], replicated, may hold values from 0 to 16383
- carbon_sites: int32 [2, 512], replicated, may hold values from 0 to 16383
- error_var: float32 [2, 512], replicated, may hold values from 32 to 256
Outputs:
- posterior: float32 [16384, 16384], P('row', 'col')
The draws below stay inside these ranges and needn't reach their ends.
Inputs may be any that keep to these rules, and one draw needn't show every extreme that they name: `ozone_sites`: cells may repeat within a batch. `carbon_sites`: cells may repeat within a batch.
All inputs are finite; a program needn't handle non-finite values.
Results may differ from the reference program's by a relative error of at most 0.00012.
Values sent between devices are 32-bit elements; how exact they have to be, the bound alone decides.
A program may use at most 192 MiB of HBM per device.

```python
import math
import jax
import jax.numpy as jnp
from jax import lax

NR = 16384
NC = 16384
K = 512
STEPS = 2
BATCHES = 2


def touch_ends(entries, own_key, least, largest):
    longest = entries.shape.index(max(entries.shape))
    spots = []
    for shift in (0, 1):
        where = [jax.random.randint(jax.random.fold_in(own_key, axis), (), 0, length) for axis, length in enumerate(entries.shape)]
        where[longest] = (where[longest] + shift) % entries.shape[longest]
        spots.append(tuple(where))
    return entries.at[spots[0]].set(least).at[spots[1]].set(largest)


def steps_of(rng, extent, cuts, smallest, top_value):
    loudness, own = 1.0, jax.random.fold_in(rng, 6)
    for dim, parts in cuts:
        heights = jnp.exp(jax.random.uniform(jax.random.fold_in(own, dim), (parts,), jnp.float32, smallest / len(cuts), top_value / len(cuts)))
        loudness = loudness * jnp.repeat(heights, extent[dim] // parts).reshape([-1 if axis == dim else 1 for axis in range(len(extent))])
    return loudness


def bell_draw(own_key, shape, spread, limit, split=(), held_as=jnp.bfloat16):
    result = spread * jax.random.normal(own_key, shape, jnp.float32)
    if split:
        result = result * steps_of(own_key, shape, split, -0.22, 0.18)
    return jnp.clip(result, -limit, limit).astype(held_as)


def setup_inputs(seed: int = 0) -> dict:
    key_of = jax.random.split(jax.random.key(seed), 11)
    prior = bell_draw(key_of[0], (NR, NC), 1.0, 6.0, ((0, 4), (1, 8)), jnp.float32)
    ozone_courant = jnp.clip(jnp.exp(jax.random.uniform(key_of[1], (NR,), jnp.float32, math.log(0.05), math.log(0.5))), 0.05, 0.5)
    ozone_diffusion = jnp.clip(jnp.exp(jax.random.uniform(key_of[2], (NR,), jnp.float32, math.log(0.02), math.log(0.25))), 0.02, 0.25)
    ozone_wind = touch_ends(jax.random.randint(key_of[3], (NR,), 0, 2), jax.random.fold_in(key_of[3], 1), 0, 1).astype(jnp.int32)
    carbon_courant = jnp.clip(jnp.exp(jax.random.uniform(key_of[4], (NC,), jnp.float32, math.log(0.05), math.log(0.5))), 0.05, 0.5)
    carbon_diffusion = jnp.clip(jnp.exp(jax.random.uniform(key_of[5], (NC,), jnp.float32, math.log(0.02), math.log(0.25))), 0.02, 0.25)
    carbon_wind = touch_ends(jax.random.randint(key_of[6], (NC,), 0, 2), jax.random.fold_in(key_of[6], 1), 0, 1).astype(jnp.int32)
    ozone_sites = touch_ends(jax.random.randint(key_of[7], (BATCHES, K), 0, NR), jax.random.fold_in(key_of[7], 1), 0, NR - 1).astype(jnp.int32)
    carbon_sites = touch_ends(jax.random.randint(key_of[8], (BATCHES, K), 0, NC), jax.random.fold_in(key_of[8], 1), 0, NC - 1).astype(jnp.int32)
    error_var = jnp.clip(jnp.exp(jax.random.uniform(key_of[9], (BATCHES, K), jnp.float32, math.log(32.0), math.log(256.0))), 32.0, 256.0)
    return dict(prior=prior, ozone_courant=ozone_courant, ozone_diffusion=ozone_diffusion, ozone_wind=ozone_wind, carbon_courant=carbon_courant, carbon_diffusion=carbon_diffusion, carbon_wind=carbon_wind, ozone_sites=ozone_sites, carbon_sites=carbon_sites, error_var=error_var)


def advance(extended, courant, diffusion, wind, dimension):
    total = extended.shape[dimension]
    before = lax.slice_in_dim(extended, 0, total - 2, axis=dimension)
    centre = lax.slice_in_dim(extended, 1, total - 1, axis=dimension)
    after = lax.slice_in_dim(extended, 2, total, axis=dimension)
    layout = (-1, 1) if dimension == 0 else (1, -1)
    upwind = jnp.where(wind.reshape(layout) == 0, before, after)
    return centre - courant.reshape(layout) * (centre - upwind) + diffusion.reshape(layout) * (before - 2.0 * centre + after)

def reference(prior, ozone_courant, ozone_diffusion, ozone_wind, carbon_courant, carbon_diffusion, carbon_wind, ozone_sites, carbon_sites, error_var):
    field = prior
    for sweep in range(STEPS):
        field = advance(jnp.pad(field, ((1, 1), (0, 0))), ozone_courant, ozone_diffusion, ozone_wind, 0)
    for sweep in range(STEPS):
        field = advance(jnp.pad(field, ((0, 0), (1, 1))), carbon_courant, carbon_diffusion, carbon_wind, 1)
    for batch in range(BATCHES):
        row_panel = field[ozone_sites[batch]]
        column_panel = field[:, carbon_sites[batch]]
        block = row_panel[:, carbon_sites[batch]]
        innovation = jnp.diag(error_var[batch]) + jnp.dot(block, block.T, precision=lax.Precision.HIGHEST)
        weights = jnp.linalg.solve(innovation, row_panel)
        field = field - jnp.dot(column_panel, weights, precision=lax.Precision.HIGHEST)
    return field
```

```python
import math
import jax
import jax.numpy as jnp
from jax import lax
from jax.experimental import pallas as pl
from jax.experimental.pallas import tpu as pltpu
from jax.sharding import PartitionSpec as P

STEPS = 2
BATCHES = 2
MARGIN = 8
LANES = 128
TILE = 128
HIGHEST = lax.Precision.HIGHEST
HIGH = lax.Precision.HIGH


def coefficients(courant, diffusion, wind, first_cell, before, after, count):
    pad = (before, after)
    total = count + before + after

    def cut(values):
        return lax.dynamic_slice_in_dim(jnp.pad(values, pad), first_cell, total)

    c, d, w = cut(courant), cut(diffusion), cut(wind)
    low = d + jnp.where(w == 0, c, 0.0)
    high = d + jnp.where(w == 0, 0.0, c)
    return low, 1.0 - c - 2.0 * d, high


def edges(value, axis, dim, width):
    size, length = lax.axis_size(axis), value.shape[dim]
    up = [(i, i + 1) for i in range(size - 1)]
    down = [(i + 1, i) for i in range(size - 1)]
    last = lax.slice_in_dim(value, length - width, length, axis=dim)
    leading = lax.slice_in_dim(value, 0, width, axis=dim)
    return lax.ppermute(last, axis, up), lax.ppermute(leading, axis, down)


def across(left, right):
    return lax.dot_general(
        left, right, (((1,), (1,)), ((), ())), preferred_element_type=jnp.float32
    )


def transport_kernel(main, prev, follow, above, below, side, row_weights, col_weights, chooser, out, *picked):
    step = pl.program_id(0)
    last = pl.num_programs(0) - 1
    top = jnp.where(step == 0, above[...], prev[...])
    bottom = jnp.where(step == last, below[...], follow[...])
    body = jnp.concatenate([top, main[...], bottom], axis=0)
    value = jnp.concatenate([body, side[0]], axis=1)
    weights = row_weights[0]
    low, mid, high = weights[:, 0:1], weights[:, 1:2], weights[:, 2:3]
    rows = value.shape[0]
    for _ in range(STEPS):
        value = low * pltpu.roll(value, 1, 0) + mid * value + high * pltpu.roll(value, rows - 1, 0)
    value = value[MARGIN : rows - MARGIN]
    width = value.shape[1]
    low, mid, high = col_weights[0:1], col_weights[1:2], col_weights[2:3]
    for _ in range(STEPS):
        value = low * pltpu.roll(value, 1, 1) + mid * value + high * pltpu.roll(value, width - 1, 1)
    value = value[:, : out.shape[1]]
    out[...] = value
    coarse = value.astype(jnp.bfloat16)
    fine = (value - coarse.astype(jnp.float32)).astype(jnp.bfloat16)
    chosen = across(chooser[...], coarse) + across(chooser[...], fine)
    count = chosen.shape[0] // len(picked)
    for index, part in enumerate(picked):
        part[...] = chosen[index * count : (index + 1) * count]


def surroundings(prior, ozone, carbon, row_first, col_first):
    rows, cols = prior.shape
    tiles, per = rows // TILE, TILE // MARGIN
    above, below = edges(prior, "row", 0, MARGIN)
    left, right = edges(prior, "col", 1, STEPS)
    strips = jnp.concatenate([right, left], axis=1)
    strip_above, strip_below = edges(strips, "row", 0, MARGIN)
    strips = jnp.concatenate([strip_above, strips, strip_below], axis=0)
    strips = jnp.concatenate(
        [
            strips[:, :STEPS],
            jnp.zeros((strips.shape[0], LANES - 2 * STEPS), jnp.float32),
            strips[:, STEPS:],
        ],
        axis=1,
    )
    extent = TILE + 2 * MARGIN

    def windows(values):
        parts = values.reshape((tiles * per + 2, MARGIN) + values.shape[1:])
        main = parts[: tiles * per].reshape((tiles, TILE) + values.shape[1:])
        tail = parts[per:].reshape((-1,) + values.shape[1:])
        tail = jnp.stack([tail[i * TILE : i * TILE + 2 * MARGIN] for i in range(tiles)])
        return jnp.concatenate([main, tail], axis=1)

    side = windows(strips)
    row_weights = windows(
        jnp.stack(coefficients(*ozone, row_first, MARGIN, MARGIN, rows), axis=1)
    )
    row_weights = jnp.pad(row_weights, ((0, 0), (0, 0), (0, 5)))
    trio = coefficients(*carbon, col_first, STEPS, STEPS, cols)
    rolled = []
    for index, entry in enumerate(trio):
        filler = jnp.zeros((LANES - 2 * STEPS,), jnp.float32)
        rolled.append(jnp.concatenate([entry[STEPS:], filler, entry[:STEPS]]))
    col_weights = jnp.pad(jnp.stack(rolled), ((0, 5), (0, 0)))
    return above, below, side, row_weights, col_weights


def transport(prior, prepared, chooser, pieces):
    rows, cols = prior.shape
    tiles, per = rows // TILE, TILE // MARGIN
    extent = TILE + 2 * MARGIN
    count = chooser.shape[0] // pieces
    blocks = rows // MARGIN
    return pl.pallas_call(
        transport_kernel,
        grid=(tiles,),
        in_specs=[
            pl.BlockSpec((TILE, cols), lambda i: (i, 0)),
            pl.BlockSpec((MARGIN, cols), lambda i: (jnp.maximum(i * per - 1, 0), 0)),
            pl.BlockSpec((MARGIN, cols), lambda i: (jnp.minimum((i + 1) * per, blocks - 1), 0)),
            pl.BlockSpec((MARGIN, cols), lambda i: (0, 0)),
            pl.BlockSpec((MARGIN, cols), lambda i: (0, 0)),
            pl.BlockSpec((1, extent, LANES), lambda i: (i, 0, 0)),
            pl.BlockSpec((1, extent, 8), lambda i: (i, 0, 0)),
            pl.BlockSpec((8, cols + LANES), lambda i: (0, 0)),
            pl.BlockSpec(chooser.shape, lambda i: (0, 0)),
        ],
        out_specs=[
            pl.BlockSpec((TILE, cols), lambda i: (i, 0)),
        ]
        + [pl.BlockSpec((count, TILE), lambda i: (0, i))] * pieces,
        out_shape=[
            jax.ShapeDtypeStruct((rows, cols), jnp.float32),
        ]
        + [jax.ShapeDtypeStruct((count, rows), jnp.float32)] * pieces,
        compiler_params=pltpu.CompilerParams(vmem_limit_bytes=60 << 20),
    )(prior, prior, prior, *prepared, chooser)


def plain(first_matrix, second_matrix):
    return jnp.dot(first_matrix, second_matrix, preferred_element_type=jnp.float32)


def rough(first_matrix, second_matrix):
    return plain(first_matrix.astype(jnp.bfloat16), second_matrix.astype(jnp.bfloat16))


def exact(first_matrix, second_matrix):
    return jnp.dot(
        first_matrix, second_matrix, precision=HIGHEST, preferred_element_type=jnp.float32
    )


def halves(value):
    coarse = value.astype(jnp.bfloat16)
    return coarse, (value - coarse.astype(jnp.float32)).astype(jnp.bfloat16)


def by_rows(count, step, write):
    def body(index, carry):
        write(pl.ds(pl.multiple_of(index * step, step), step))
        return carry

    lax.fori_loop(0, count // step, body, 0)


def chunk(count):
    return 128 if count % 128 == 0 else 16


def below(rows, first):
    return pl.ds(rows.start + first, rows.size)


def unit_rows(rows, k):
    down = lax.broadcasted_iota(jnp.int32, (rows.size, k), 0) + rows.start
    return (down == lax.broadcasted_iota(jnp.int32, (rows.size, k), 1)).astype(jnp.float32)


def cut(parts, value, rows=slice(None)):
    for index in range(parts.shape[0]):
        term = value.astype(jnp.bfloat16)
        parts[index, rows, :] = term
        value = value - term.astype(jnp.float32)


def joined(left, right, rows, product=plain):
    small = product(left[0, rows, :], right[2]) + product(left[2, rows, :], right[0])
    small += product(left[1, rows, :], right[1])
    small += product(left[0, rows, :], right[1]) + product(left[1, rows, :], right[0])
    return small + product(left[0, rows, :], right[0])


def whole_call(kernel, outs, scratch, *args, cost):
    whole = pl.BlockSpec(memory_space=pltpu.VMEM)
    return pl.pallas_call(
        kernel,
        in_specs=[whole] * len(args),
        out_specs=[whole] * len(outs),
        out_shape=[jax.ShapeDtypeStruct(*out) for out in outs],
        scratch_shapes=[pltpu.VMEM(*entry) for entry in scratch],
        cost_estimate=pl.CostEstimate(
            flops=int(cost * 9e8), bytes_accessed=1 << 20, transcendentals=0
        ),
        compiler_params=pltpu.CompilerParams(vmem_limit_bytes=60 << 20),
    )(*args)


def assemble_kernel(slotted, place, g, parts):
    cut(parts, slotted[...])

    def write(rows):
        picks = place[rows, :]
        g[rows, :] = plain(picks, parts[0]) + plain(picks, parts[1]) + plain(picks, parts[2])

    by_rows(g.shape[0], chunk(g.shape[0]), write)
    g[...] = g[...].T


def invert_kernel(block, variance, x, s, sp, xp, ep):
    k = s.shape[0]
    step = chunk(k)
    cut(xp, block[...])

    def innovation(rows):
        s[rows, :] = unit_rows(rows, k) * variance[...] + joined(xp, xp, rows, across)

    by_rows(k, step, innovation)
    cut(sp, s[...])
    bound = jnp.max(jnp.sum(jnp.abs(s[...]), axis=0))

    def begin():
        x[...] = (1.0 / bound) * unit_rows(pl.ds(0, k), k)
        cut(xp, x[...])

    def residual(precise):
        def body(index, total):
            rows = pl.ds(pl.multiple_of(index * step, step), step)
            if precise:
                left = unit_rows(rows, k) - joined(sp, xp, rows)
                cut(ep, left, rows)
            else:
                left = unit_rows(rows, k) - plain(sp[0, rows, :], xp[0])
                ep[0, rows, :] = left.astype(jnp.bfloat16)
            return total + jnp.sum(left * left)

        return lax.fori_loop(0, k // step, body, jnp.float32(0.0))

    def improve(precise):
        def write(rows):
            value = plain(xp[0, rows, :], ep[0])
            if precise:
                value += plain(xp[0, rows, :], ep[1]) + plain(xp[1, rows, :], ep[0])
            value += x[rows, :]
            x[rows, :] = value
            if precise:
                cut(xp, value, rows)
            else:
                xp[0, rows, :] = value.astype(jnp.bfloat16)

        by_rows(k, step, write)

    begin()
    first = residual(False)

    def coarse_more(state):
        index, norm = state
        return (index < 14) & (norm > 0.25) & (norm <= 1.1 * first)

    def coarse_step(state):
        index, _ = state
        improve(False)
        return index + 1, residual(False)

    lax.while_loop(coarse_more, coarse_step, (jnp.int32(0), first))
    cut(xp, x[...])

    def fine_more(state):
        index, norm = state
        return (index < 60) & jnp.logical_not(norm < 1e-7)

    def fine_step(state):
        index, norm = state

        @pl.when((index == 0) | (norm < 0.8) | (index > 1))
        def _():
            @pl.when(index > 0)
            def _():
                improve(True)

        @pl.when((index == 1) & jnp.logical_not(norm < 0.8))
        def _():
            begin()

        return index + 1, residual(True)

    lax.while_loop(fine_more, fine_step, (jnp.int32(0), jnp.float32(1.0)))
    improve(True)


def deflate_kernel(g, x0, carry, block, left, right):
    k = x0.shape[0]
    step = chunk(k)
    cut(left, g[k:, :k])
    cut(right, x0[...])

    def carry_rows(rows):
        carry[rows, :] = joined(left, right, rows)

    by_rows(k, step, carry_rows)
    cut(left, carry[...])
    cut(right, g[:k, k:])

    def block_rows(rows):
        block[rows, :] = g[below(rows, k), k:] - joined(left, right, rows)

    by_rows(k, step, block_rows)


def gain_kernel(g, x0, x1, carry, spots, back, coarse_out, fine_out, hp, ap, xp, tp, part):
    k = x0.shape[0]
    step = chunk(k)
    both = 2 * k
    low, high = pl.ds(0, k), pl.ds(k, k)

    def put(rows, columns, value):
        coarse, fine = halves(value)
        part[0, rows, columns] = coarse
        part[1, rows, columns] = fine

    cut(hp, x0[...])
    cut(ap, g[:k, k:])

    def h_rows(rows):
        cut(xp, joined(hp, ap, rows), rows)

    by_rows(k, step, h_rows)
    for index in range(3):
        hp[index] = xp[index]
    cut(xp, x1[...])

    def right_rows(rows):
        put(rows, high, -joined(hp, xp, rows))
        put(below(rows, k), high, x1[rows, :])

    by_rows(k, step, right_rows)

    def a_rows(rows):
        value = joined(xp, ap, rows)
        put(below(rows, k), low, -value)
        cut(tp, value, rows)

    cut(ap, carry[...])
    by_rows(k, step, a_rows)

    def left_rows(rows):
        put(rows, low, x0[rows, :] + joined(hp, tp, rows))

    by_rows(k, step, left_rows)

    def slot_rows(rows):
        picks = back[rows, :]
        for index, out in ((0, coarse_out), (1, fine_out)):
            moved = plain(picks, part[index]).astype(jnp.bfloat16)
            out[rows, :] = plain(moved, spots[...]).astype(jnp.bfloat16)

    by_rows(back.shape[0], chunk(back.shape[0]), slot_rows)


def gain(slotted, place, spots, back, variance):
    slots, both = slotted.shape
    k = both // 2
    square = ((k, k), jnp.float32)
    terms = ((3, k, k), jnp.bfloat16)
    (g,) = whole_call(
        assemble_kernel,
        [((both, both), jnp.float32)],
        [((3, slots, both), jnp.bfloat16)],
        slotted,
        place,
        cost=15,
    )

    def inverse(block, b):
        scratch = [square, terms, terms, terms]
        return whole_call(
            invert_kernel, [square], scratch, block, variance[b : b + 1], cost=30
        )[0]

    x0 = inverse(g[:k, :k], 0)
    carry, block = whole_call(deflate_kernel, [square, square], [terms, terms], g, x0, cost=8)
    x1 = inverse(block, 1)
    out = ((slots, spots.shape[1]), jnp.bfloat16)
    return whole_call(
        gain_kernel,
        [out, out],
        [terms] * 4 + [((2, both, both), jnp.bfloat16)],
        g,
        x0,
        x1,
        carry,
        spots,
        back,
        cost=28,
    )


def crossing_kernel(known, slotted, send, recv, side_send, side_recv):
    size = lax.axis_size("col")
    half, side = known.shape[0] // 2, known.shape[1] // 2
    row, col = lax.axis_index("row"), lax.axis_index("col")
    core = row % 2
    even = col % 2 == 0
    ahead = jnp.where(
        even,
        jnp.where(col + 2 < size, col + 2, col + 1),
        jnp.where(col > 1, col - 2, col - 1),
    )
    behind = jnp.where(
        even,
        jnp.where(col > 1, col - 2, col + 1),
        jnp.where(col + 2 < size, col + 2, col - 1),
    )
    partner = row + 1 - 2 * core
    mesh_ids = pl.DeviceIdType.MESH
    barrier = pltpu.get_barrier_semaphore()
    for device in ({"col": ahead}, {"col": behind}, {"row": partner}):
        pl.semaphore_signal(barrier, inc=1, device_id=device, device_id_type=mesh_ids)
    pl.semaphore_wait(barrier, 3)
    columns = pl.ds(pl.multiple_of(core * side, side), side)

    def slot(way, step):
        return slotted.at[pl.ds((way * size + step) * half, half), columns]

    def source(way, step):
        if step == 0:
            return known.at[pl.ds(way * half, half), columns]
        return slot(way, step)

    copies, sides = {}, []
    for step in range(size):
        for way, device in ((0, {"col": ahead}), (1, {"col": behind})):
            if step:
                copies[way, step - 1].wait_recv()
            if step < size - 1:
                copy = pltpu.make_async_remote_copy(
                    src_ref=source(way, step),
                    dst_ref=slot(way, step + 1),
                    send_sem=send.at[way, step],
                    recv_sem=recv.at[way, step],
                    device_id=device,
                    device_id_type=mesh_ids,
                )
                copy.start()
                copies[way, step] = copy
            copy = pltpu.make_async_remote_copy(
                src_ref=source(way, step),
                dst_ref=slot(way, step),
                send_sem=side_send.at[way, step],
                recv_sem=side_recv.at[way, step],
                device_id={"row": partner},
                device_id_type=mesh_ids,
            )
            copy.start()
            sides.append(copy)
            if step == 0:
                slotted[pl.ds(way * size * half, half), columns] = known[
                    pl.ds(way * half, half), columns
                ]
    for copy in copies.values():
        copy.wait_send()
    for copy in sides:
        copy.wait()


def crossing_gather(known):
    size = lax.axis_size("col")
    whole = pl.BlockSpec(memory_space=pltpu.VMEM)
    sems = pltpu.SemaphoreType.DMA((2, size))
    return pl.pallas_call(
        crossing_kernel,
        in_specs=[whole],
        out_specs=whole,
        out_shape=jax.ShapeDtypeStruct((known.shape[0] * size, known.shape[1]), known.dtype),
        scratch_shapes=[sems] * 4,
        compiler_params=pltpu.CompilerParams(collective_id=0, has_side_effects=True),
    )(known)


def weights_kernel(gain_coarse, gain_fine, *refs):
    panels, (coarse_out, fine_out) = refs[:-2], refs[-2:]
    coarse, fine = halves(jnp.concatenate([panel[...] for panel in panels], axis=0))

    def write(rows):
        value = plain(gain_coarse[rows, :], coarse)
        value += plain(gain_coarse[rows, :], fine) + plain(gain_fine[rows, :], coarse)
        coarse_out[rows, :], fine_out[rows, :] = halves(value)

    by_rows(gain_coarse.shape[0], 16 * (gain_coarse.shape[0] // 64), write)


def weights_of(gain_coarse, gain_fine, panels):
    slots = gain_coarse.shape[0]
    cols = panels[0].shape[1]
    wide = min(256, cols)
    held = pl.BlockSpec(gain_coarse.shape, lambda j: (0, 0), pipeline_mode=pl.Buffered(1))
    out = jax.ShapeDtypeStruct((slots, cols), jnp.bfloat16)
    return pl.pallas_call(
        weights_kernel,
        grid=(cols // wide,),
        in_specs=[held, held]
        + [pl.BlockSpec((p.shape[0], wide), lambda j: (0, j)) for p in panels],
        out_specs=[pl.BlockSpec((slots, wide), lambda j: (0, j))] * 2,
        out_shape=[out, out],
        cost_estimate=pl.CostEstimate(
            flops=6 * slots * gain_coarse.shape[1] * cols,
            bytes_accessed=12 * slots * cols,
            transcendentals=0,
        ),
        compiler_params=pltpu.CompilerParams(vmem_limit_bytes=60 << 20),
    )(gain_coarse, gain_fine, *panels)


def update_kernel(field, weights_coarse, weights_fine, *refs):
    panels, out = refs[:-1], refs[-1]
    panel = jnp.concatenate([part[...] for part in panels], axis=0).T
    coarse, fine = halves(panel)
    wide = min(512, out.shape[1])
    for first in range(0, out.shape[1], wide):
        columns = slice(first, first + wide)
        value = plain(coarse, weights_coarse[:, columns])
        value += plain(coarse, weights_fine[:, columns])
        value += plain(fine, weights_coarse[:, columns])
        out[:, columns] = field[:, columns] - value


def update(field, weights_coarse, weights_fine, panels):
    rows, cols = field.shape
    tall = min(256, rows)
    tile = pl.BlockSpec((tall, cols), lambda i: (i, 0))
    held = pl.BlockSpec(weights_coarse.shape, lambda i: (0, 0), pipeline_mode=pl.Buffered(1))
    return pl.pallas_call(
        update_kernel,
        grid=(rows // tall,),
        in_specs=[tile, held, held]
        + [pl.BlockSpec((p.shape[0], tall), lambda i: (0, i)) for p in panels],
        out_specs=tile,
        out_shape=jax.ShapeDtypeStruct(field.shape, jnp.float32),
        compiler_params=pltpu.CompilerParams(vmem_limit_bytes=60 << 20),
    )(field, weights_coarse, weights_fine, *panels)


def capacity(total, parts):
    mean = total / parts
    need = math.ceil((mean + 3.0 * math.sqrt(mean * (1 - 1 / parts))) / 16) * 16
    return min(need, total)


def ring_of(size):
    return list(range(0, size, 2)) + list(range(size - 1 - size % 2, 0, -2))


def ring_gather(up_part, down_part, axis):
    cycle = ring_of(lax.axis_size(axis))
    ahead = [(cycle[i], cycle[(i + 1) % len(cycle)]) for i in range(len(cycle))]
    behind = [(b, a) for a, b in ahead]
    ups, downs = [up_part], [down_part]
    for _ in range(len(cycle) - 1):
        ups.append(lax.ppermute(ups[-1], axis, ahead))
        downs.append(lax.ppermute(downs[-1], axis, behind))
    return ups, downs


def doubling_masks(size):
    masks, reach = [0], size // 2
    while reach:
        masks += [mask ^ reach for mask in masks]
        reach //= 2
    return masks


def doubling_gather(value, axis):
    size = lax.axis_size(axis)
    parts, reach = [value], size // 2
    while reach:
        pairs = [(i, i ^ reach) for i in range(size)]
        parts += [lax.ppermute(part, axis, pairs) for part in parts]
        reach //= 2
    return parts


def lookup(table, index):
    return jnp.sum(
        jnp.where(index[:, None] == jnp.arange(len(table))[None, :], jnp.array(table)[None, :], 0),
        axis=1,
    )


def places(sites, extent):
    owner = sites // extent
    before = jnp.tril(jnp.ones((sites.size, sites.size), jnp.bool_), -1)
    same = owner[:, None] == owner[None, :]
    return owner, jnp.sum((same & before).astype(jnp.int32), axis=1)


def local_cells(sites, owner, rank, me, extent, count, empty):
    hit = (owner == me)[None, :] & (rank[None, :] == jnp.arange(count)[:, None])
    cell = jnp.sum(jnp.where(hit, (sites - me * extent - empty)[None, :], 0), axis=1)
    return cell + empty


def one_hot(index, count):
    return (index[:, None] == jnp.arange(count)[None, :]).astype(jnp.bfloat16)


def pick_rows(matrix, sites, first_cell):
    count = matrix.shape[0]
    offsets = sites - first_cell
    owned = (offsets >= 0) & (offsets < count)
    picked = matrix[jnp.clip(offsets, 0, count - 1)]
    return jnp.where(owned[:, None], picked, 0.0)


def balanced(prior, prepared, row_sites, col_sites, error_var, row_place, col_place):
    rows, cols = prior.shape
    across_rows, across_cols = lax.axis_size("row"), lax.axis_size("col")
    my_row, my_col = lax.axis_index("row"), lax.axis_index("col")
    total = row_sites.size
    row_slots, col_slots = capacity(total, across_rows), capacity(total, across_cols)
    row_owner, row_rank = row_place
    col_owner, col_rank = col_place
    half = col_slots // 2

    my_rows = local_cells(row_sites, row_owner, row_rank, my_row, rows, row_slots, 0)
    my_cols = local_cells(col_sites, col_owner, col_rank, my_col, cols, col_slots, -1)
    chooser = one_hot(my_cols, cols)

    masks = doubling_masks(across_rows)
    order = [masks.index(mask) for mask in range(across_rows)]
    row_slot = lookup(order, row_owner ^ my_row) * row_slots + row_rank
    cycle = ring_of(across_cols)
    spot = [cycle.index(c) for c in range(across_cols)]
    here = lookup(spot, my_col[None])[0]
    away = lookup(spot, col_owner) - here
    up_step, down_step = (-away) % across_cols, away % across_cols
    col_slot = jnp.where(
        col_rank < half,
        up_step * half + col_rank,
        (across_cols + down_step) * half + col_rank - half,
    )
    spots = one_hot(row_slot, across_rows * row_slots)
    place = one_hot(col_slot, across_cols * col_slots)

    field, up_part, down_part = transport(prior, prepared, chooser, 2)
    row_part = field[my_rows]
    crossing = lax.dot_general(
        chooser.astype(jnp.float32), row_part, (((1,), (1,)), ((), ())), precision=HIGHEST
    )
    pieces = doubling_gather(crossing, "row")
    known = exact(jnp.concatenate(pieces, axis=1), spots.astype(jnp.float32).T)
    slotted = crossing_gather(known)
    panels = doubling_gather(row_part, "row")
    up_panels, down_panels = ring_gather(up_part, down_part, "col")
    gain_coarse, gain_fine = gain(slotted, place, spots, place.T, error_var)
    weights = weights_of(gain_coarse, gain_fine, panels)
    return update(field, *weights, up_panels + down_panels)


def crowded(prior, prepared, row_sites, col_sites, error_var, row_place, col_place):
    rows, cols = prior.shape
    row_first = lax.axis_index("row") * rows
    col_first = lax.axis_index("col") * cols
    chooser = one_hot(col_sites - col_first, cols)
    field, picked = transport(prior, prepared, chooser, 1)
    row_part = pick_rows(field, row_sites, row_first)
    crossing = lax.dot_general(
        chooser.astype(jnp.float32), row_part, (((1,), (1,)), ((), ())), precision=HIGHEST
    )
    crossing = lax.psum(crossing, ("row", "col"))
    row_panel = lax.psum(row_part, "row")
    column_panel = lax.psum(picked, "col")
    same = jnp.eye(row_sites.size, dtype=jnp.bfloat16)
    weights = weights_of(*gain(crossing, same, same, same, error_var), [row_panel])
    return update(field, *weights, [column_panel])


def shards(
    prior,
    ozone_courant,
    ozone_diffusion,
    ozone_wind,
    carbon_courant,
    carbon_diffusion,
    carbon_wind,
    ozone_sites,
    carbon_sites,
    error_var,
):
    rows, cols = prior.shape
    row_sites = ozone_sites.reshape(-1)
    col_sites = carbon_sites.reshape(-1)
    ozone = (ozone_courant, ozone_diffusion, ozone_wind)
    carbon = (carbon_courant, carbon_diffusion, carbon_wind)
    row_place = places(row_sites, rows)
    col_place = places(col_sites, cols)
    total = row_sites.size
    fits = (jnp.max(row_place[1]) < capacity(total, lax.axis_size("row"))) & (
        jnp.max(col_place[1]) < capacity(total, lax.axis_size("col"))
    )
    prepared = surroundings(
        prior, ozone, carbon, lax.axis_index("row") * rows, lax.axis_index("col") * cols
    )
    given = (prior, prepared, row_sites, col_sites, error_var, row_place, col_place)
    return lax.cond(fits, balanced, crowded, *given)


def solution(mesh):
    placed = (P("row", "col"), P(), P(), P(), P(), P(), P(), P(), P(), P())
    return jax.shard_map(
        shards, mesh=mesh, in_specs=placed, out_specs=P("row", "col"), check_vma=False
    )
```

```python
import math
import jax
import jax.numpy as jnp
from jax import lax
from jax.experimental import pallas as pl
from jax.experimental.pallas import tpu as pltpu
from jax.sharding import PartitionSpec as P

STEPS = 2
BATCHES = 2
MARGIN = 8
LANES = 128
TILE = 128
HIGHEST = lax.Precision.HIGHEST
LAST = 4
SCALE = 1.5


def coefficients(courant, diffusion, wind, first_cell, before, after, count):
    pad = (before, after)
    total = count + before + after

    def cut(values):
        return lax.dynamic_slice_in_dim(jnp.pad(values, pad), first_cell, total)

    c, d, w = cut(courant), cut(diffusion), cut(wind)
    low = d + jnp.where(w == 0, c, 0.0)
    high = d + jnp.where(w == 0, 0.0, c)
    return low, 1.0 - c - 2.0 * d, high


def edges(value, axis, dim, width):
    size, length = lax.axis_size(axis), value.shape[dim]
    up = [(i, i + 1) for i in range(size - 1)]
    down = [(i + 1, i) for i in range(size - 1)]
    last = lax.slice_in_dim(value, length - width, length, axis=dim)
    leading = lax.slice_in_dim(value, 0, width, axis=dim)
    return lax.ppermute(last, axis, up), lax.ppermute(leading, axis, down)


def across(left, right):
    return lax.dot_general(
        left, right, (((1,), (1,)), ((), ())), preferred_element_type=jnp.float32
    )


def transport_kernel(main, prev, follow, above, below, side, row_weights, col_weights, chooser, out, *picked):
    step = pl.program_id(0)
    last = pl.num_programs(0) - 1
    top = jnp.where(step == 0, above[...], prev[...])
    bottom = jnp.where(step == last, below[...], follow[...])
    body = jnp.concatenate([top, main[...], bottom], axis=0)
    value = jnp.concatenate([body, side[0]], axis=1)
    weights = row_weights[0]
    low, mid, high = weights[:, 0:1], weights[:, 1:2], weights[:, 2:3]
    rows = value.shape[0]
    for _ in range(STEPS):
        value = low * pltpu.roll(value, 1, 0) + mid * value + high * pltpu.roll(value, rows - 1, 0)
    value = value[MARGIN : rows - MARGIN]
    width = value.shape[1]
    low, mid, high = col_weights[0:1], col_weights[1:2], col_weights[2:3]
    for _ in range(STEPS):
        value = low * pltpu.roll(value, 1, 1) + mid * value + high * pltpu.roll(value, width - 1, 1)
    value = value[:, : out.shape[1]]
    out[...] = value
    coarse = value.astype(jnp.bfloat16)
    fine = (value - coarse.astype(jnp.float32)).astype(jnp.bfloat16)
    chosen = across(chooser[...], coarse) + across(chooser[...], fine)
    count = chosen.shape[0] // len(picked)
    for index, part in enumerate(picked):
        part[...] = chosen[index * count : (index + 1) * count]


def surroundings(prior, ozone, carbon, row_first, col_first):
    rows, cols = prior.shape
    tiles, per = rows // TILE, TILE // MARGIN
    above, below = edges(prior, "row", 0, MARGIN)
    left, right = edges(prior, "col", 1, STEPS)
    strips = jnp.concatenate([right, left], axis=1)
    strip_above, strip_below = edges(strips, "row", 0, MARGIN)
    strips = jnp.concatenate([strip_above, strips, strip_below], axis=0)
    strips = jnp.concatenate(
        [
            strips[:, :STEPS],
            jnp.zeros((strips.shape[0], LANES - 2 * STEPS), jnp.float32),
            strips[:, STEPS:],
        ],
        axis=1,
    )
    extent = TILE + 2 * MARGIN

    def windows(values):
        parts = values.reshape((tiles * per + 2, MARGIN) + values.shape[1:])
        main = parts[: tiles * per].reshape((tiles, TILE) + values.shape[1:])
        tail = parts[per:].reshape((-1,) + values.shape[1:])
        tail = jnp.stack([tail[i * TILE : i * TILE + 2 * MARGIN] for i in range(tiles)])
        return jnp.concatenate([main, tail], axis=1)

    side = windows(strips)
    row_weights = windows(
        jnp.stack(coefficients(*ozone, row_first, MARGIN, MARGIN, rows), axis=1)
    )
    row_weights = jnp.pad(row_weights, ((0, 0), (0, 0), (0, 5)))
    trio = coefficients(*carbon, col_first, STEPS, STEPS, cols)
    rolled = []
    for index, entry in enumerate(trio):
        filler = jnp.zeros((LANES - 2 * STEPS,), jnp.float32)
        rolled.append(jnp.concatenate([entry[STEPS:], filler, entry[:STEPS]]))
    col_weights = jnp.pad(jnp.stack(rolled), ((0, 5), (0, 0)))
    return above, below, side, row_weights, col_weights


def transport(prior, prepared, chooser, pieces):
    rows, cols = prior.shape
    tiles, per = rows // TILE, TILE // MARGIN
    extent = TILE + 2 * MARGIN
    count = chooser.shape[0] // pieces
    blocks = rows // MARGIN
    return pl.pallas_call(
        transport_kernel,
        grid=(tiles,),
        in_specs=[
            pl.BlockSpec((TILE, cols), lambda i: (i, 0)),
            pl.BlockSpec((MARGIN, cols), lambda i: (jnp.maximum(i * per - 1, 0), 0)),
            pl.BlockSpec((MARGIN, cols), lambda i: (jnp.minimum((i + 1) * per, blocks - 1), 0)),
            pl.BlockSpec((MARGIN, cols), lambda i: (0, 0)),
            pl.BlockSpec((MARGIN, cols), lambda i: (0, 0)),
            pl.BlockSpec((1, extent, LANES), lambda i: (i, 0, 0)),
            pl.BlockSpec((1, extent, 8), lambda i: (i, 0, 0)),
            pl.BlockSpec((8, cols + LANES), lambda i: (0, 0)),
            pl.BlockSpec(chooser.shape, lambda i: (0, 0)),
        ],
        out_specs=[
            pl.BlockSpec((TILE, cols), lambda i: (i, 0)),
        ]
        + [pl.BlockSpec((count, TILE), lambda i: (0, i))] * pieces,
        out_shape=[
            jax.ShapeDtypeStruct((rows, cols), jnp.float32),
        ]
        + [jax.ShapeDtypeStruct((count, rows), jnp.float32)] * pieces,
        compiler_params=pltpu.CompilerParams(vmem_limit_bytes=60 << 20),
    )(prior, prior, prior, *prepared, chooser)


def plain(first_matrix, second_matrix):
    return jnp.dot(first_matrix, second_matrix, preferred_element_type=jnp.float32)


def rough(first_matrix, second_matrix):
    return plain(first_matrix.astype(jnp.bfloat16), second_matrix.astype(jnp.bfloat16))


def exact(first_matrix, second_matrix):
    return jnp.dot(
        first_matrix, second_matrix, precision=HIGHEST, preferred_element_type=jnp.float32
    )


def halves(value):
    coarse = value.astype(jnp.bfloat16)
    return coarse, (value - coarse.astype(jnp.float32)).astype(jnp.bfloat16)


def by_rows(count, step, write):
    def body(index, carry):
        write(pl.ds(pl.multiple_of(index * step, step), step))
        return carry

    lax.fori_loop(0, count // step, body, 0)


def chunk(count):
    return 128 if count % 128 == 0 else 16


def below(rows, first):
    return pl.ds(rows.start + first, rows.size)


def unit_rows(rows, k):
    down = lax.broadcasted_iota(jnp.int32, (rows.size, k), 0) + rows.start
    return (down == lax.broadcasted_iota(jnp.int32, (rows.size, k), 1)).astype(jnp.float32)


def cut(parts, value, rows=slice(None)):
    for index in range(parts.shape[0]):
        term = value.astype(jnp.bfloat16)
        parts[index, rows, :] = term
        value = value - term.astype(jnp.float32)


def joined(left, right, rows, product=plain):
    small = product(left[0, rows, :], right[2]) + product(left[2, rows, :], right[0])
    small += product(left[1, rows, :], right[1])
    small += product(left[0, rows, :], right[1]) + product(left[1, rows, :], right[0])
    return small + product(left[0, rows, :], right[0])


def whole_call(kernel, outs, scratch, *args, cost):
    whole = pl.BlockSpec(memory_space=pltpu.VMEM)
    return pl.pallas_call(
        kernel,
        in_specs=[whole] * len(args),
        out_specs=[whole] * len(outs),
        out_shape=[jax.ShapeDtypeStruct(*out) for out in outs],
        scratch_shapes=[pltpu.VMEM(*entry) for entry in scratch],
        cost_estimate=pl.CostEstimate(
            flops=int(cost * SCALE * 1e9), bytes_accessed=1 << 20, transcendentals=0
        ),
        compiler_params=pltpu.CompilerParams(vmem_limit_bytes=60 << 20),
    )(*args)


def assemble_kernel(slotted, place, g, parts):
    cut(parts, slotted[...])

    def write(rows):
        picks = place[rows, :]
        g[rows, :] = plain(picks, parts[0]) + plain(picks, parts[1]) + plain(picks, parts[2])

    by_rows(g.shape[0], chunk(g.shape[0]), write)
    g[...] = g[...].T


def invert_kernel(block, variance, x, s, sp, xp, ep):
    k = s.shape[0]
    step = chunk(k)
    cut(xp, block[...])

    def innovation(rows):
        s[rows, :] = unit_rows(rows, k) * variance[...] + joined(xp, xp, rows, across)

    by_rows(k, step, innovation)
    cut(sp, s[...])
    bound = jnp.max(jnp.sum(jnp.abs(s[...]), axis=0))

    def begin():
        x[...] = (1.0 / bound) * unit_rows(pl.ds(0, k), k)
        cut(xp, x[...])

    def residual(precise):
        def body(index, total):
            rows = pl.ds(pl.multiple_of(index * step, step), step)
            if precise:
                left = unit_rows(rows, k) - joined(sp, xp, rows)
                cut(ep, left, rows)
            else:
                left = unit_rows(rows, k) - plain(sp[0, rows, :], xp[0])
                ep[0, rows, :] = left.astype(jnp.bfloat16)
            return total + jnp.sum(left * left)

        return lax.fori_loop(0, k // step, body, jnp.float32(0.0))

    def improve(precise):
        def write(rows):
            value = plain(xp[0, rows, :], ep[0])
            if precise:
                value += plain(xp[0, rows, :], ep[1]) + plain(xp[1, rows, :], ep[0])
            value += x[rows, :]
            x[rows, :] = value
            if precise:
                cut(xp, value, rows)
            else:
                xp[0, rows, :] = value.astype(jnp.bfloat16)

        by_rows(k, step, write)

    begin()
    first = residual(False)

    def coarse_more(state):
        index, norm = state
        return (index < 14) & (norm > 0.25) & (norm <= 1.1 * first)

    def coarse_step(state):
        index, _ = state
        improve(False)
        return index + 1, residual(False)

    lax.while_loop(coarse_more, coarse_step, (jnp.int32(0), first))
    cut(xp, x[...])

    def fine_more(state):
        index, norm = state
        return (index < 60) & jnp.logical_not(norm < 1e-5)

    def fine_step(state):
        index, norm = state

        @pl.when((index == 0) | (norm < 0.8) | (index > 1))
        def _():
            @pl.when(index > 0)
            def _():
                improve(True)

        @pl.when((index == 1) & jnp.logical_not(norm < 0.8))
        def _():
            begin()

        return index + 1, residual(True)

    lax.while_loop(fine_more, fine_step, (jnp.int32(0), jnp.float32(1.0)))
    improve(True)


def deflate_kernel(g, x0, carry, block, left, right):
    k = x0.shape[0]
    step = chunk(k)
    cut(left, g[k:, :k])
    cut(right, x0[...])

    def carry_rows(rows):
        carry[rows, :] = joined(left, right, rows)

    by_rows(k, step, carry_rows)
    cut(left, carry[...])
    cut(right, g[:k, k:])

    def block_rows(rows):
        block[rows, :] = g[below(rows, k), k:] - joined(left, right, rows)

    by_rows(k, step, block_rows)


def gain_kernel(g, x0, x1, carry, spots, back, coarse_out, fine_out, hp, ap, xp, tp, part):
    k = x0.shape[0]
    step = chunk(k)
    both = 2 * k
    low, high = pl.ds(0, k), pl.ds(k, k)

    def put(rows, columns, value):
        coarse, fine = halves(value)
        part[0, rows, columns] = coarse
        part[1, rows, columns] = fine

    cut(hp, x0[...])
    cut(ap, g[:k, k:])

    def h_rows(rows):
        cut(xp, joined(hp, ap, rows), rows)

    by_rows(k, step, h_rows)
    for index in range(3):
        hp[index] = xp[index]
    cut(xp, x1[...])

    def right_rows(rows):
        put(rows, high, -joined(hp, xp, rows))
        put(below(rows, k), high, x1[rows, :])

    by_rows(k, step, right_rows)

    def a_rows(rows):
        value = joined(xp, ap, rows)
        put(below(rows, k), low, -value)
        cut(tp, value, rows)

    cut(ap, carry[...])
    by_rows(k, step, a_rows)

    def left_rows(rows):
        put(rows, low, x0[rows, :] + joined(hp, tp, rows))

    by_rows(k, step, left_rows)

    def slot_rows(rows):
        picks = back[rows, :]
        for index, out in ((0, coarse_out), (1, fine_out)):
            moved = plain(picks, part[index]).astype(jnp.bfloat16)
            out[rows, :] = plain(moved, spots[...]).astype(jnp.bfloat16)

    by_rows(back.shape[0], chunk(back.shape[0]), slot_rows)


def gain(slotted, place, spots, back, variance):
    slots, both = slotted.shape
    k = both // 2
    square = ((k, k), jnp.float32)
    terms = ((3, k, k), jnp.bfloat16)
    (g,) = whole_call(
        assemble_kernel,
        [((both, both), jnp.float32)],
        [((3, slots, both), jnp.bfloat16)],
        slotted,
        place,
        cost=15,
    )

    def inverse(block, b):
        scratch = [square, terms, terms, terms]
        return whole_call(
            invert_kernel, [square], scratch, block, variance[b : b + 1], cost=30
        )[0]

    x0 = inverse(g[:k, :k], 0)
    carry, block = whole_call(deflate_kernel, [square, square], [terms, terms], g, x0, cost=8)
    x1 = inverse(block, 1)
    out = ((slots, spots.shape[1]), jnp.bfloat16)
    return whole_call(
        gain_kernel,
        [out, out],
        [terms] * 4 + [((2, both, both), jnp.bfloat16)],
        g,
        x0,
        x1,
        carry,
        spots,
        back,
        cost=28,
    )


def crossing_kernel(known, slotted, send, recv, side_send, side_recv):
    size = lax.axis_size("col")
    half, side = known.shape[0] // 2, known.shape[1] // 2
    row, col = lax.axis_index("row"), lax.axis_index("col")
    core = row % 2
    even = col % 2 == 0
    ahead = jnp.where(
        even,
        jnp.where(col + 2 < size, col + 2, col + 1),
        jnp.where(col > 1, col - 2, col - 1),
    )
    behind = jnp.where(
        even,
        jnp.where(col > 1, col - 2, col + 1),
        jnp.where(col + 2 < size, col + 2, col - 1),
    )
    partner = row + 1 - 2 * core
    mesh_ids = pl.DeviceIdType.MESH
    barrier = pltpu.get_barrier_semaphore()
    for device in ({"col": ahead}, {"col": behind}, {"row": partner}):
        pl.semaphore_signal(barrier, inc=1, device_id=device, device_id_type=mesh_ids)
    pl.semaphore_wait(barrier, 3)
    columns = pl.ds(pl.multiple_of(core * side, side), side)

    def slot(way, step):
        return slotted.at[pl.ds((2 * step + way) * half, half), columns]

    def source(way, step):
        if step == 0:
            return known.at[pl.ds(way * half, half), columns]
        return slot(way, step)

    copies, sides = {}, []
    for step in range(size):
        for way, device in ((0, {"col": ahead}), (1, {"col": behind})):
            if step:
                copies[way, step - 1].wait_recv()
            if step < size - 1:
                copy = pltpu.make_async_remote_copy(
                    src_ref=source(way, step),
                    dst_ref=slot(way, step + 1),
                    send_sem=send.at[way, step],
                    recv_sem=recv.at[way, step],
                    device_id=device,
                    device_id_type=mesh_ids,
                )
                copy.start()
                copies[way, step] = copy
            copy = pltpu.make_async_remote_copy(
                src_ref=source(way, step),
                dst_ref=slot(way, step),
                send_sem=side_send.at[way, step],
                recv_sem=side_recv.at[way, step],
                device_id={"row": partner},
                device_id_type=mesh_ids,
            )
            copy.start()
            sides.append(copy)
            if step == 0:
                slotted[pl.ds(way * half, half), columns] = known[
                    pl.ds(way * half, half), columns
                ]
    for copy in copies.values():
        copy.wait_send()
    for copy in sides:
        copy.wait()


def crossing_gather(known):
    size = lax.axis_size("col")
    whole = pl.BlockSpec(memory_space=pltpu.VMEM)
    sems = pltpu.SemaphoreType.DMA((2, size))
    return pl.pallas_call(
        crossing_kernel,
        in_specs=[whole],
        out_specs=whole,
        out_shape=jax.ShapeDtypeStruct((known.shape[0] * size, known.shape[1]), known.dtype),
        scratch_shapes=[sems] * 4,
        compiler_params=pltpu.CompilerParams(collective_id=0, has_side_effects=True),
    )(known)


def weights_kernel(gain_coarse, gain_fine, *refs):
    panels, (coarse_out, fine_out) = refs[:-2], refs[-2:]
    coarse, fine = halves(jnp.concatenate([panel[...] for panel in panels], axis=0))

    def write(rows):
        value = plain(gain_coarse[rows, :], coarse)
        value += plain(gain_coarse[rows, :], fine) + plain(gain_fine[rows, :], coarse)
        coarse_out[rows, :], fine_out[rows, :] = halves(value)

    by_rows(gain_coarse.shape[0], 16 * (gain_coarse.shape[0] // 64), write)


def weights_of(gain_coarse, gain_fine, panels):
    slots = gain_coarse.shape[0]
    cols = panels[0].shape[1]
    wide = min(256, cols)
    held = pl.BlockSpec(gain_coarse.shape, lambda j: (0, 0), pipeline_mode=pl.Buffered(1))
    out = jax.ShapeDtypeStruct((slots, cols), jnp.bfloat16)
    return pl.pallas_call(
        weights_kernel,
        grid=(cols // wide,),
        in_specs=[held, held]
        + [pl.BlockSpec((p.shape[0], wide), lambda j: (0, j)) for p in panels],
        out_specs=[pl.BlockSpec((slots, wide), lambda j: (0, j))] * 2,
        out_shape=[out, out],
        cost_estimate=pl.CostEstimate(
            flops=6 * slots * gain_coarse.shape[1] * cols,
            bytes_accessed=12 * slots * cols,
            transcendentals=0,
        ),
        compiler_params=pltpu.CompilerParams(vmem_limit_bytes=60 << 20),
    )(gain_coarse, gain_fine, *panels)


def update_kernel(field, weights_coarse, weights_fine, *refs):
    panels, out = refs[:-1], refs[-1]
    panel = jnp.concatenate([part[...] for part in panels], axis=0).T
    coarse, fine = halves(panel)
    wide = min(512, out.shape[1])

    def body(index, carry):
        columns = pl.ds(pl.multiple_of(index * wide, wide), wide)
        value = plain(coarse, weights_coarse[:, columns])
        value += plain(coarse, weights_fine[:, columns])
        value += plain(fine, weights_coarse[:, columns])
        out[:, columns] = field[:, columns] - value
        return carry

    lax.fori_loop(0, out.shape[1] // wide, body, 0)


def update(field, weights_coarse, weights_fine, panels, piece):
    rows, cols = field.shape
    tall = min(256, rows)
    tile = pl.BlockSpec((tall, cols), lambda i: (i, 0))
    slots = len(panels) * panels[0].shape[0]
    held = pl.BlockSpec((slots, cols), lambda i: (piece, 0), pipeline_mode=pl.Buffered(1))
    return pl.pallas_call(
        update_kernel,
        grid=(rows // tall,),
        in_specs=[tile, held, held]
        + [pl.BlockSpec((p.shape[0], tall), lambda i: (0, i)) for p in panels],
        out_specs=tile,
        out_shape=jax.ShapeDtypeStruct(field.shape, jnp.float32),
        cost_estimate=pl.CostEstimate(
            flops=8 * slots * rows * cols, bytes_accessed=8 * rows * cols, transcendentals=0
        ),
        compiler_params=pltpu.CompilerParams(vmem_limit_bytes=60 << 20),
    )(field, weights_coarse, weights_fine, *panels)


def capacity(total, parts):
    mean = total / parts
    need = math.ceil((mean + 3.0 * math.sqrt(mean * (1 - 1 / parts))) / 16) * 16
    return min(need, total)


def ring_of(size):
    return list(range(0, size, 2)) + list(range(size - 1 - size % 2, 0, -2))


def ring_gather(up_part, down_part, axis, after):
    cycle = ring_of(lax.axis_size(axis))
    ahead = [(cycle[i], cycle[(i + 1) % len(cycle)]) for i in range(len(cycle))]
    behind = [(b, a) for a, b in ahead]
    ups, downs = [up_part], [down_part]
    for _ in range(len(cycle) - 1):
        ups.append(lax.ppermute(ups[-1], axis, ahead))
        downs.append(lax.ppermute(downs[-1], axis, behind))
        if len(ups) == 2:
            ups[1], downs[1], after = lax.optimization_barrier((ups[1], downs[1], after))
    return [part for pair in zip(ups, downs) for part in pair], after


def doubling_masks(size):
    masks, reach = [0], size // 2
    while reach:
        masks += [mask ^ reach for mask in masks]
        reach //= 2
    return masks


def doubling_gather(value, axis):
    size = lax.axis_size(axis)
    parts, reach = [value], size // 2
    while reach:
        pairs = [(i, i ^ reach) for i in range(size)]
        parts += [lax.ppermute(part, axis, pairs) for part in parts]
        reach //= 2
    return parts


def lookup(table, index):
    return jnp.sum(
        jnp.where(index[:, None] == jnp.arange(len(table))[None, :], jnp.array(table)[None, :], 0),
        axis=1,
    )


def places(sites, extent):
    owner = sites // extent
    before = jnp.tril(jnp.ones((sites.size, sites.size), jnp.bool_), -1)
    same = owner[:, None] == owner[None, :]
    return owner, jnp.sum((same & before).astype(jnp.int32), axis=1)


def local_cells(sites, owner, rank, me, extent, count, empty):
    hit = (owner == me)[None, :] & (rank[None, :] == jnp.arange(count)[:, None])
    cell = jnp.sum(jnp.where(hit, (sites - me * extent - empty)[None, :], 0), axis=1)
    return cell + empty


def one_hot(index, count):
    return (index[:, None] == jnp.arange(count)[None, :]).astype(jnp.bfloat16)


def pick_rows(matrix, sites, first_cell):
    count = matrix.shape[0]
    offsets = sites - first_cell
    owned = (offsets >= 0) & (offsets < count)
    picked = matrix[jnp.clip(offsets, 0, count - 1)]
    return jnp.where(owned[:, None], picked, 0.0)


def balanced(prior, prepared, row_sites, col_sites, error_var, row_place, col_place):
    rows, cols = prior.shape
    across_rows, across_cols = lax.axis_size("row"), lax.axis_size("col")
    my_row, my_col = lax.axis_index("row"), lax.axis_index("col")
    total = row_sites.size
    row_slots, col_slots = capacity(total, across_rows), capacity(total, across_cols)
    row_owner, row_rank = row_place
    col_owner, col_rank = col_place
    half = col_slots // 2

    my_rows = local_cells(row_sites, row_owner, row_rank, my_row, rows, row_slots, 0)
    my_cols = local_cells(col_sites, col_owner, col_rank, my_col, cols, col_slots, -1)
    chooser = one_hot(my_cols, cols)

    masks = doubling_masks(across_rows)
    order = [masks.index(mask) for mask in range(across_rows)]
    row_slot = lookup(order, row_owner ^ my_row) * row_slots + row_rank
    cycle = ring_of(across_cols)
    spot = [cycle.index(c) for c in range(across_cols)]
    here = lookup(spot, my_col[None])[0]
    away = lookup(spot, col_owner) - here
    up_step, down_step = (-away) % across_cols, away % across_cols
    col_slot = jnp.where(
        col_rank < half,
        2 * up_step * half + col_rank,
        2 * down_step * half + col_rank,
    )
    spots = one_hot(row_slot, across_rows * row_slots)
    place = one_hot(col_slot, across_cols * col_slots)

    field, up_part, down_part = transport(prior, prepared, chooser, 2)
    row_part = field[my_rows]
    crossing = lax.dot_general(
        chooser.astype(jnp.float32), row_part, (((1,), (1,)), ((), ())), precision=HIGHEST
    )
    pieces = doubling_gather(crossing, "row")
    known = exact(jnp.concatenate(pieces, axis=1), spots.astype(jnp.float32).T)
    row_part, known = lax.optimization_barrier((row_part, known))
    slotted = crossing_gather(known)
    panels = doubling_gather(row_part, "row")
    parts, slotted = ring_gather(up_part, down_part, "col", slotted)
    gain_coarse, gain_fine = gain(slotted, place, spots, place.T, error_var)
    weights = weights_of(gain_coarse, gain_fine, panels)
    last = len(parts) // LAST
    field = update(field, *weights, parts[:-last], 0)
    return update(field, *weights, parts[-last:], LAST - 1)


def added_up(value, axis):
    size, reach = lax.axis_size(axis), 1
    while reach < size:
        pairs = [(i, i ^ reach) for i in range(size)]
        value = value + lax.ppermute(value, axis, pairs)
        reach *= 2
    return value


def product_kernel(left, right, out):
    out[...] = exact(left[...], right[...])


def product(left, right):
    (rows, depth), cols = left.shape, right.shape[1]
    tall, wide = min(128, rows), min(128, cols)
    return pl.pallas_call(
        product_kernel,
        grid=(rows // tall, cols // wide),
        in_specs=[
            pl.BlockSpec((tall, depth), lambda i, j: (i, 0)),
            pl.BlockSpec((depth, wide), lambda i, j: (0, j)),
        ],
        out_specs=pl.BlockSpec((tall, wide), lambda i, j: (i, j)),
        out_shape=jax.ShapeDtypeStruct((rows, cols), jnp.float32),
    )(left, right)


def newton(matrix):
    unit = jnp.eye(matrix.shape[0], dtype=jnp.float32)

    def more(state):
        index, _, norm = state
        return (index < 60) & jnp.logical_not(norm < 1e-7)

    def step(state):
        index, inverse, _ = state
        error = unit - product(matrix, inverse)
        return index + 1, inverse + product(inverse, error), jnp.sum(error * error)

    inverse = unit / jnp.max(jnp.sum(jnp.abs(matrix), axis=0))
    return lax.while_loop(more, step, (jnp.int32(0), inverse, jnp.float32(1.0)))[1]


def crowded(prior, prepared, row_sites, col_sites, error_var, row_place, col_place):
    rows, cols = prior.shape
    row_first = lax.axis_index("row") * rows
    col_first = lax.axis_index("col") * cols
    k = error_var.shape[1]
    chooser = one_hot(col_sites - col_first, cols)
    field, picked = transport(prior, prepared, chooser, 1)
    row_part = pick_rows(field, row_sites, row_first)
    crossing = product(row_part, chooser.astype(jnp.float32).T)
    crossing = added_up(added_up(crossing, "row"), "col")
    row_panel = added_up(row_part, "row")
    column_panel = added_up(picked, "col")

    def body(b, state):
        crossing, row_panel, column_panel, field = state
        mine = b * k
        block = lax.dynamic_slice(crossing, (mine, mine), (k, k))
        variance = lax.dynamic_index_in_dim(error_var, b, 0, keepdims=False)
        inverse = newton(jnp.diag(variance) + product(block, block.T))
        picked_rows = lax.dynamic_slice_in_dim(row_panel, mine, k, axis=0)
        picked_cols = lax.dynamic_slice_in_dim(column_panel, mine, k, axis=0).T
        weights = product(inverse, picked_rows)
        field = field - product(picked_cols, weights)
        cross_rows = lax.dynamic_slice_in_dim(crossing, mine, k, axis=0)
        cross_cols = lax.dynamic_slice_in_dim(crossing, mine, k, axis=1)
        row_panel = row_panel - product(cross_cols, weights)
        gains = product(inverse, cross_rows)
        column_panel = column_panel - product(gains.T, picked_cols.T)
        return crossing - product(cross_cols, gains), row_panel, column_panel, field

    state = (crossing, row_panel, column_panel, field)
    return lax.fori_loop(0, error_var.shape[0], body, state)[3]


def shards(
    prior,
    ozone_courant,
    ozone_diffusion,
    ozone_wind,
    carbon_courant,
    carbon_diffusion,
    carbon_wind,
    ozone_sites,
    carbon_sites,
    error_var,
):
    rows, cols = prior.shape
    row_sites = ozone_sites.reshape(-1)
    col_sites = carbon_sites.reshape(-1)
    ozone = (ozone_courant, ozone_diffusion, ozone_wind)
    carbon = (carbon_courant, carbon_diffusion, carbon_wind)
    row_place = places(row_sites, rows)
    col_place = places(col_sites, cols)
    total = row_sites.size
    fits = (jnp.max(row_place[1]) < capacity(total, lax.axis_size("row"))) & (
        jnp.max(col_place[1]) < capacity(total, lax.axis_size("col"))
    )
    prepared = surroundings(
        prior, ozone, carbon, lax.axis_index("row") * rows, lax.axis_index("col") * cols
    )
    given = (prior, prepared, row_sites, col_sites, error_var, row_place, col_place)
    return lax.cond(fits, balanced, crowded, *given)


def solution(mesh):
    placed = (P("row", "col"), P(), P(), P(), P(), P(), P(), P(), P(), P())
    return jax.shard_map(
        shards, mesh=mesh, in_specs=placed, out_specs=P("row", "col"), check_vma=False
    )
```

```python
import math
import jax
import jax.numpy as jnp
from jax import lax
from jax.experimental import pallas as pl
from jax.experimental.pallas import tpu as pltpu
from jax.sharding import PartitionSpec as P

STEPS = 2
BATCHES = 2
MARGIN = 8
LANES = 128
TILE = 128
HIGHEST = lax.Precision.HIGHEST
LAST = 4
SCALE = 1.5


def coefficients(courant, diffusion, wind, first_cell, before, after, count):
    pad = (before, after)
    total = count + before + after

    def cut(values):
        return lax.dynamic_slice_in_dim(jnp.pad(values, pad), first_cell, total)

    c, d, w = cut(courant), cut(diffusion), cut(wind)
    low = d + jnp.where(w == 0, c, 0.0)
    high = d + jnp.where(w == 0, 0.0, c)
    return low, 1.0 - c - 2.0 * d, high


def edges(value, axis, dim, width):
    size, length = lax.axis_size(axis), value.shape[dim]
    up = [(i, i + 1) for i in range(size - 1)]
    down = [(i + 1, i) for i in range(size - 1)]
    last = lax.slice_in_dim(value, length - width, length, axis=dim)
    leading = lax.slice_in_dim(value, 0, width, axis=dim)
    return lax.ppermute(last, axis, up), lax.ppermute(leading, axis, down)


def across(left, right):
    return lax.dot_general(
        left, right, (((1,), (1,)), ((), ())), preferred_element_type=jnp.float32
    )


def transport_kernel(main, prev, follow, above, below, side, row_weights, col_weights, chooser, out, *picked):
    step = pl.program_id(0)
    last = pl.num_programs(0) - 1
    top = jnp.where(step == 0, above[...], prev[...])
    bottom = jnp.where(step == last, below[...], follow[...])
    body = jnp.concatenate([top, main[...], bottom], axis=0)
    value = jnp.concatenate([body, side[0]], axis=1)
    weights = row_weights[0]
    low, mid, high = weights[:, 0:1], weights[:, 1:2], weights[:, 2:3]
    rows = value.shape[0]
    for _ in range(STEPS):
        value = low * pltpu.roll(value, 1, 0) + mid * value + high * pltpu.roll(value, rows - 1, 0)
    value = value[MARGIN : rows - MARGIN]
    width = value.shape[1]
    low, mid, high = col_weights[0:1], col_weights[1:2], col_weights[2:3]
    for _ in range(STEPS):
        value = low * pltpu.roll(value, 1, 1) + mid * value + high * pltpu.roll(value, width - 1, 1)
    value = value[:, : out.shape[1]]
    out[...] = value
    coarse = value.astype(jnp.bfloat16)
    fine = (value - coarse.astype(jnp.float32)).astype(jnp.bfloat16)
    chosen = across(chooser[...], coarse) + across(chooser[...], fine)
    count = chosen.shape[0] // len(picked)
    for index, part in enumerate(picked):
        part[...] = chosen[index * count : (index + 1) * count]


def surroundings(prior, ozone, carbon, row_first, col_first):
    rows, cols = prior.shape
    tiles, per = rows // TILE, TILE // MARGIN
    above, below = edges(prior, "row", 0, MARGIN)
    left, right = edges(prior, "col", 1, STEPS)
    strips = jnp.concatenate([right, left], axis=1)
    strip_above, strip_below = edges(strips, "row", 0, MARGIN)
    strips = jnp.concatenate([strip_above, strips, strip_below], axis=0)
    strips = jnp.concatenate(
        [
            strips[:, :STEPS],
            jnp.zeros((strips.shape[0], LANES - 2 * STEPS), jnp.float32),
            strips[:, STEPS:],
        ],
        axis=1,
    )
    extent = TILE + 2 * MARGIN

    def windows(values):
        parts = values.reshape((tiles * per + 2, MARGIN) + values.shape[1:])
        main = parts[: tiles * per].reshape((tiles, TILE) + values.shape[1:])
        tail = parts[per:].reshape((-1,) + values.shape[1:])
        tail = jnp.stack([tail[i * TILE : i * TILE + 2 * MARGIN] for i in range(tiles)])
        return jnp.concatenate([main, tail], axis=1)

    side = windows(strips)
    row_weights = windows(
        jnp.stack(coefficients(*ozone, row_first, MARGIN, MARGIN, rows), axis=1)
    )
    row_weights = jnp.pad(row_weights, ((0, 0), (0, 0), (0, 5)))
    trio = coefficients(*carbon, col_first, STEPS, STEPS, cols)
    rolled = []
    for index, entry in enumerate(trio):
        filler = jnp.zeros((LANES - 2 * STEPS,), jnp.float32)
        rolled.append(jnp.concatenate([entry[STEPS:], filler, entry[:STEPS]]))
    col_weights = jnp.pad(jnp.stack(rolled), ((0, 5), (0, 0)))
    return above, below, side, row_weights, col_weights


def transport(prior, prepared, chooser, pieces):
    rows, cols = prior.shape
    tiles, per = rows // TILE, TILE // MARGIN
    extent = TILE + 2 * MARGIN
    count = chooser.shape[0] // pieces
    blocks = rows // MARGIN
    return pl.pallas_call(
        transport_kernel,
        grid=(tiles,),
        in_specs=[
            pl.BlockSpec((TILE, cols), lambda i: (i, 0)),
            pl.BlockSpec((MARGIN, cols), lambda i: (jnp.maximum(i * per - 1, 0), 0)),
            pl.BlockSpec((MARGIN, cols), lambda i: (jnp.minimum((i + 1) * per, blocks - 1), 0)),
            pl.BlockSpec((MARGIN, cols), lambda i: (0, 0)),
            pl.BlockSpec((MARGIN, cols), lambda i: (0, 0)),
            pl.BlockSpec((1, extent, LANES), lambda i: (i, 0, 0)),
            pl.BlockSpec((1, extent, 8), lambda i: (i, 0, 0)),
            pl.BlockSpec((8, cols + LANES), lambda i: (0, 0)),
            pl.BlockSpec(chooser.shape, lambda i: (0, 0)),
        ],
        out_specs=[
            pl.BlockSpec((TILE, cols), lambda i: (i, 0)),
        ]
        + [pl.BlockSpec((count, TILE), lambda i: (0, i))] * pieces,
        out_shape=[
            jax.ShapeDtypeStruct((rows, cols), jnp.float32),
        ]
        + [jax.ShapeDtypeStruct((count, rows), jnp.float32)] * pieces,
        compiler_params=pltpu.CompilerParams(vmem_limit_bytes=60 << 20),
    )(prior, prior, prior, *prepared, chooser)


def plain(first_matrix, second_matrix):
    return jnp.dot(first_matrix, second_matrix, preferred_element_type=jnp.float32)


def rough(first_matrix, second_matrix):
    return plain(first_matrix.astype(jnp.bfloat16), second_matrix.astype(jnp.bfloat16))


def exact(first_matrix, second_matrix):
    return jnp.dot(
        first_matrix, second_matrix, precision=HIGHEST, preferred_element_type=jnp.float32
    )


def halves(value):
    coarse = value.astype(jnp.bfloat16)
    return coarse, (value - coarse.astype(jnp.float32)).astype(jnp.bfloat16)


def by_rows(count, step, write):
    def body(index, carry):
        write(pl.ds(pl.multiple_of(index * step, step), step))
        return carry

    lax.fori_loop(0, count // step, body, 0)


def chunk(count):
    return next(n for n in (512, 640, 256, 128, 16) if count % n == 0)


def below(rows, first):
    return pl.ds(rows.start + first, rows.size)


def unit_rows(rows, k):
    down = lax.broadcasted_iota(jnp.int32, (rows.size, k), 0) + rows.start
    return (down == lax.broadcasted_iota(jnp.int32, (rows.size, k), 1)).astype(jnp.float32)


def cut(parts, value, rows=slice(None)):
    for index in range(parts.shape[0]):
        term = value.astype(jnp.bfloat16)
        parts[index, rows, :] = term
        value = value - term.astype(jnp.float32)


def joined(left, right, rows, product=plain):
    small = product(left[0, rows, :], right[2]) + product(left[2, rows, :], right[0])
    small += product(left[1, rows, :], right[1])
    small += product(left[0, rows, :], right[1]) + product(left[1, rows, :], right[0])
    return small + product(left[0, rows, :], right[0])


def whole_call(kernel, outs, scratch, *args, cost):
    whole = pl.BlockSpec(memory_space=pltpu.VMEM)
    return pl.pallas_call(
        kernel,
        in_specs=[whole] * len(args),
        out_specs=[whole] * len(outs),
        out_shape=[jax.ShapeDtypeStruct(*out) for out in outs],
        scratch_shapes=[pltpu.VMEM(*entry) for entry in scratch],
        cost_estimate=pl.CostEstimate(
            flops=int(cost * SCALE * 1e9), bytes_accessed=1 << 20, transcendentals=0
        ),
        compiler_params=pltpu.CompilerParams(vmem_limit_bytes=60 << 20),
    )(*args)


def assemble_kernel(slotted, place, g, parts):
    cut(parts, slotted[...])

    def write(rows):
        picks = place[rows, :]
        g[rows, :] = plain(picks, parts[0]) + plain(picks, parts[1]) + plain(picks, parts[2])

    by_rows(g.shape[0], chunk(g.shape[0]), write)
    g[...] = g[...].T


def invert_kernel(block, variance, x, s, sp, xp, ep):
    k = s.shape[0]
    step = chunk(k)
    cut(xp, block[...])

    def innovation(rows):
        s[rows, :] = unit_rows(rows, k) * variance[...] + joined(xp, xp, rows, across)

    by_rows(k, step, innovation)
    cut(sp, s[...])
    bound = jnp.max(jnp.sum(jnp.abs(s[...]), axis=0))

    def begin():
        x[...] = (1.0 / bound) * unit_rows(pl.ds(0, k), k)
        cut(xp, x[...])

    def residual(precise):
        def body(index, total):
            rows = pl.ds(pl.multiple_of(index * step, step), step)
            if precise:
                left = unit_rows(rows, k) - joined(sp, xp, rows)
                cut(ep, left, rows)
            else:
                left = unit_rows(rows, k) - plain(sp[0, rows, :], xp[0])
                ep[0, rows, :] = left.astype(jnp.bfloat16)
            return total + jnp.sum(left * left)

        return lax.fori_loop(0, k // step, body, jnp.float32(0.0))

    def improve(precise):
        def write(rows):
            value = plain(xp[0, rows, :], ep[0])
            if precise:
                value += plain(xp[0, rows, :], ep[1]) + plain(xp[1, rows, :], ep[0])
            value += x[rows, :]
            x[rows, :] = value
            if precise:
                cut(xp, value, rows)
            else:
                xp[0, rows, :] = value.astype(jnp.bfloat16)

        by_rows(k, step, write)

    begin()
    first = residual(False)

    def coarse_more(state):
        index, norm = state
        return (index < 14) & (norm > 0.25) & (norm <= 1.1 * first)

    def coarse_step(state):
        index, _ = state
        improve(False)
        return index + 1, residual(False)

    lax.while_loop(coarse_more, coarse_step, (jnp.int32(0), first))
    cut(xp, x[...])

    def fine_more(state):
        index, norm = state
        return (index < 60) & jnp.logical_not(norm < 1e-5)

    def fine_step(state):
        index, norm = state

        @pl.when((index == 0) | (norm < 0.8) | (index > 1))
        def _():
            @pl.when(index > 0)
            def _():
                improve(True)

        @pl.when((index == 1) & jnp.logical_not(norm < 0.8))
        def _():
            begin()

        return index + 1, residual(True)

    lax.while_loop(fine_more, fine_step, (jnp.int32(0), jnp.float32(1.0)))
    improve(True)


def deflate_kernel(g, x0, carry, block, left, right):
    k = x0.shape[0]
    step = chunk(k)
    cut(left, g[k:, :k])
    cut(right, x0[...])

    def carry_rows(rows):
        carry[rows, :] = joined(left, right, rows)

    by_rows(k, step, carry_rows)
    cut(left, carry[...])
    cut(right, g[:k, k:])

    def block_rows(rows):
        block[rows, :] = g[below(rows, k), k:] - joined(left, right, rows)

    by_rows(k, step, block_rows)


def gain_kernel(g, x0, x1, carry, spots, back, coarse_out, fine_out, hp, ap, xp, tp, part):
    k = x0.shape[0]
    step = chunk(k)
    both = 2 * k
    low, high = pl.ds(0, k), pl.ds(k, k)

    def put(rows, columns, value):
        coarse, fine = halves(value)
        part[0, rows, columns] = coarse
        part[1, rows, columns] = fine

    cut(hp, x0[...])
    cut(ap, g[:k, k:])

    def h_rows(rows):
        cut(xp, joined(hp, ap, rows), rows)

    by_rows(k, step, h_rows)
    for index in range(3):
        hp[index] = xp[index]
    cut(xp, x1[...])

    def right_rows(rows):
        put(rows, high, -joined(hp, xp, rows))
        put(below(rows, k), high, x1[rows, :])

    by_rows(k, step, right_rows)

    def a_rows(rows):
        value = joined(xp, ap, rows)
        put(below(rows, k), low, -value)
        cut(tp, value, rows)

    cut(ap, carry[...])
    by_rows(k, step, a_rows)

    def left_rows(rows):
        put(rows, low, x0[rows, :] + joined(hp, tp, rows))

    by_rows(k, step, left_rows)

    def slot_rows(rows):
        picks = back[rows, :]
        for index, out in ((0, coarse_out), (1, fine_out)):
            moved = plain(picks, part[index]).astype(jnp.bfloat16)
            out[rows, :] = plain(moved, spots[...]).astype(jnp.bfloat16)

    by_rows(back.shape[0], chunk(back.shape[0]), slot_rows)


def gain(slotted, place, spots, back, variance):
    slots, both = slotted.shape
    k = both // 2
    square = ((k, k), jnp.float32)
    terms = ((3, k, k), jnp.bfloat16)
    (g,) = whole_call(
        assemble_kernel,
        [((both, both), jnp.float32)],
        [((3, slots, both), jnp.bfloat16)],
        slotted,
        place,
        cost=17,
    )

    def inverse(block, b):
        scratch = [square, terms, terms, terms]
        return whole_call(
            invert_kernel, [square], scratch, block, variance[b : b + 1], cost=21
        )[0]

    x0 = inverse(g[:k, :k], 0)
    carry, block = whole_call(deflate_kernel, [square, square], [terms, terms], g, x0, cost=7)
    x1 = inverse(block, 1)
    out = ((slots, spots.shape[1]), jnp.bfloat16)
    return whole_call(
        gain_kernel,
        [out, out],
        [terms] * 4 + [((2, both, both), jnp.bfloat16)],
        g,
        x0,
        x1,
        carry,
        spots,
        back,
        cost=26,
    )


def crossing_kernel(known, slotted, send, recv, side_send, side_recv):
    size = lax.axis_size("col")
    half, side = known.shape[0] // 2, known.shape[1] // 2
    row, col = lax.axis_index("row"), lax.axis_index("col")
    core = row % 2
    even = col % 2 == 0
    ahead = jnp.where(
        even,
        jnp.where(col + 2 < size, col + 2, col + 1),
        jnp.where(col > 1, col - 2, col - 1),
    )
    behind = jnp.where(
        even,
        jnp.where(col > 1, col - 2, col + 1),
        jnp.where(col + 2 < size, col + 2, col - 1),
    )
    partner = row + 1 - 2 * core
    mesh_ids = pl.DeviceIdType.MESH
    barrier = pltpu.get_barrier_semaphore()
    for device in ({"col": ahead}, {"col": behind}, {"row": partner}):
        pl.semaphore_signal(barrier, inc=1, device_id=device, device_id_type=mesh_ids)
    pl.semaphore_wait(barrier, 3)
    columns = pl.ds(pl.multiple_of(core * side, side), side)

    def slot(way, step):
        return slotted.at[pl.ds((2 * step + way) * half, half), columns]

    def source(way, step):
        if step == 0:
            return known.at[pl.ds(way * half, half), columns]
        return slot(way, step)

    copies, sides = {}, []
    for step in range(size):
        for way, device in ((0, {"col": ahead}), (1, {"col": behind})):
            if step:
                copies[way, step - 1].wait_recv()
            if step < size - 1:
                copy = pltpu.make_async_remote_copy(
                    src_ref=source(way, step),
                    dst_ref=slot(way, step + 1),
                    send_sem=send.at[way, step],
                    recv_sem=recv.at[way, step],
                    device_id=device,
                    device_id_type=mesh_ids,
                )
                copy.start()
                copies[way, step] = copy
            copy = pltpu.make_async_remote_copy(
                src_ref=source(way, step),
                dst_ref=slot(way, step),
                send_sem=side_send.at[way, step],
                recv_sem=side_recv.at[way, step],
                device_id={"row": partner},
                device_id_type=mesh_ids,
            )
            copy.start()
            sides.append(copy)
            if step == 0:
                slotted[pl.ds(way * half, half), columns] = known[
                    pl.ds(way * half, half), columns
                ]
    for copy in copies.values():
        copy.wait_send()
    for copy in sides:
        copy.wait()


def crossing_gather(known):
    size = lax.axis_size("col")
    whole = pl.BlockSpec(memory_space=pltpu.VMEM)
    sems = pltpu.SemaphoreType.DMA((2, size))
    return pl.pallas_call(
        crossing_kernel,
        in_specs=[whole],
        out_specs=whole,
        out_shape=jax.ShapeDtypeStruct((known.shape[0] * size, known.shape[1]), known.dtype),
        scratch_shapes=[sems] * 4,
        compiler_params=pltpu.CompilerParams(collective_id=0, has_side_effects=True),
    )(known)


def weights_kernel(gain_coarse, gain_fine, *refs):
    panels, (coarse_out, fine_out) = refs[:-2], refs[-2:]
    coarse, fine = halves(jnp.concatenate([panel[...] for panel in panels], axis=0))

    def write(rows):
        value = plain(gain_coarse[rows, :], coarse)
        value += plain(gain_coarse[rows, :], fine) + plain(gain_fine[rows, :], coarse)
        coarse_out[rows, :], fine_out[rows, :] = halves(value)

    by_rows(gain_coarse.shape[0], gain_coarse.shape[0], write)


def weights_of(gain_coarse, gain_fine, panels):
    slots = gain_coarse.shape[0]
    cols = panels[0].shape[1]
    wide = min(256, cols)
    held = pl.BlockSpec(gain_coarse.shape, lambda j: (0, 0), pipeline_mode=pl.Buffered(1))
    out = jax.ShapeDtypeStruct((slots, cols), jnp.bfloat16)
    return pl.pallas_call(
        weights_kernel,
        grid=(cols // wide,),
        in_specs=[held, held]
        + [pl.BlockSpec((p.shape[0], wide), lambda j: (0, j)) for p in panels],
        out_specs=[pl.BlockSpec((slots, wide), lambda j: (0, j))] * 2,
        out_shape=[out, out],
        cost_estimate=pl.CostEstimate(
            flops=6 * slots * gain_coarse.shape[1] * cols,
            bytes_accessed=12 * slots * cols,
            transcendentals=0,
        ),
        compiler_params=pltpu.CompilerParams(vmem_limit_bytes=60 << 20),
    )(gain_coarse, gain_fine, *panels)


def update_kernel(field, weights_coarse, weights_fine, *refs):
    panels, out = refs[:-1], refs[-1]
    panel = jnp.concatenate([part[...] for part in panels], axis=0).T
    coarse, fine = halves(panel)
    wide = min(512, out.shape[1])

    for index in range(out.shape[1] // wide):
        columns = pl.ds(index * wide, wide)
        value = plain(coarse, weights_coarse[:, columns])
        value += plain(coarse, weights_fine[:, columns])
        value += plain(fine, weights_coarse[:, columns])
        out[:, columns] = field[:, columns] - value


def update(field, weights_coarse, weights_fine, panels, piece):
    rows, cols = field.shape
    tall = min(256, rows)
    tile = pl.BlockSpec((tall, cols), lambda i: (i, 0))
    slots = len(panels) * panels[0].shape[0]
    held = pl.BlockSpec((slots, cols), lambda i: (piece, 0), pipeline_mode=pl.Buffered(1))
    return pl.pallas_call(
        update_kernel,
        grid=(rows // tall,),
        in_specs=[tile, held, held]
        + [pl.BlockSpec((p.shape[0], tall), lambda i: (0, i)) for p in panels],
        out_specs=tile,
        out_shape=jax.ShapeDtypeStruct(field.shape, jnp.float32),
        cost_estimate=pl.CostEstimate(
            flops=8 * slots * rows * cols, bytes_accessed=8 * rows * cols, transcendentals=0
        ),
        compiler_params=pltpu.CompilerParams(vmem_limit_bytes=60 << 20),
    )(field, weights_coarse, weights_fine, *panels)


def capacity(total, parts):
    mean = total / parts
    need = math.ceil((mean + 3.0 * math.sqrt(mean * (1 - 1 / parts))) / 16) * 16
    return min(need, total)


def ring_of(size):
    return list(range(0, size, 2)) + list(range(size - 1 - size % 2, 0, -2))


def ring_gather(up_part, down_part, axis, after):
    cycle = ring_of(lax.axis_size(axis))
    ahead = [(cycle[i], cycle[(i + 1) % len(cycle)]) for i in range(len(cycle))]
    behind = [(b, a) for a, b in ahead]
    ups, downs = [up_part], [down_part]
    for _ in range(len(cycle) - 1):
        ups.append(lax.ppermute(ups[-1], axis, ahead))
        downs.append(lax.ppermute(downs[-1], axis, behind))
        if len(ups) == 2:
            ups[1], downs[1], after = lax.optimization_barrier((ups[1], downs[1], after))
    return [part for pair in zip(ups, downs) for part in pair], after


def doubling_masks(size):
    masks, reach = [0], size // 2
    while reach:
        masks += [mask ^ reach for mask in masks]
        reach //= 2
    return masks


def doubling_gather(value, axis):
    size = lax.axis_size(axis)
    parts, reach = [value], size // 2
    while reach:
        pairs = [(i, i ^ reach) for i in range(size)]
        parts += [lax.ppermute(part, axis, pairs) for part in parts]
        reach //= 2
    return parts


def lookup(table, index):
    return jnp.sum(
        jnp.where(index[:, None] == jnp.arange(len(table))[None, :], jnp.array(table)[None, :], 0),
        axis=1,
    )


def places(sites, extent):
    owner = sites // extent
    before = jnp.tril(jnp.ones((sites.size, sites.size), jnp.bool_), -1)
    same = owner[:, None] == owner[None, :]
    return owner, jnp.sum((same & before).astype(jnp.int32), axis=1)


def local_cells(sites, owner, rank, me, extent, count, empty):
    hit = (owner == me)[None, :] & (rank[None, :] == jnp.arange(count)[:, None])
    cell = jnp.sum(jnp.where(hit, (sites - me * extent - empty)[None, :], 0), axis=1)
    return cell + empty


def one_hot(index, count):
    return (index[:, None] == jnp.arange(count)[None, :]).astype(jnp.bfloat16)


def pick_rows(matrix, sites, first_cell):
    count = matrix.shape[0]
    offsets = sites - first_cell
    owned = (offsets >= 0) & (offsets < count)
    picked = matrix[jnp.clip(offsets, 0, count - 1)]
    return jnp.where(owned[:, None], picked, 0.0)


def balanced(prior, prepared, row_sites, col_sites, error_var, row_place, col_place):
    rows, cols = prior.shape
    across_rows, across_cols = lax.axis_size("row"), lax.axis_size("col")
    my_row, my_col = lax.axis_index("row"), lax.axis_index("col")
    total = row_sites.size
    row_slots, col_slots = capacity(total, across_rows), capacity(total, across_cols)
    row_owner, row_rank = row_place
    col_owner, col_rank = col_place
    half = col_slots // 2

    my_rows = local_cells(row_sites, row_owner, row_rank, my_row, rows, row_slots, 0)
    my_cols = local_cells(col_sites, col_owner, col_rank, my_col, cols, col_slots, -1)
    chooser = one_hot(my_cols, cols)

    masks = doubling_masks(across_rows)
    order = [masks.index(mask) for mask in range(across_rows)]
    row_slot = lookup(order, row_owner ^ my_row) * row_slots + row_rank
    cycle = ring_of(across_cols)
    spot = [cycle.index(c) for c in range(across_cols)]
    here = lookup(spot, my_col[None])[0]
    away = lookup(spot, col_owner) - here
    up_step, down_step = (-away) % across_cols, away % across_cols
    col_slot = jnp.where(
        col_rank < half,
        2 * up_step * half + col_rank,
        2 * down_step * half + col_rank,
    )
    spots = one_hot(row_slot, across_rows * row_slots)
    place = one_hot(col_slot, across_cols * col_slots)

    field, up_part, down_part = transport(prior, prepared, chooser, 2)
    row_part = field[my_rows]
    crossing = lax.dot_general(
        chooser.astype(jnp.float32), row_part, (((1,), (1,)), ((), ())), precision=HIGHEST
    )
    pieces = doubling_gather(crossing, "row")
    known = exact(jnp.concatenate(pieces, axis=1), spots.astype(jnp.float32).T)
    row_part, known = lax.optimization_barrier((row_part, known))
    slotted = crossing_gather(known)
    panels = doubling_gather(row_part, "row")
    parts, slotted = ring_gather(up_part, down_part, "col", slotted)
    gain_coarse, gain_fine = gain(slotted, place, spots, place.T, error_var)
    weights = weights_of(gain_coarse, gain_fine, panels)
    last = len(parts) // LAST
    field = update(field, *weights, parts[:-last], 0)
    return update(field, *weights, parts[-last:], LAST - 1)


def added_up(value, axis):
    size, reach = lax.axis_size(axis), 1
    while reach < size:
        pairs = [(i, i ^ reach) for i in range(size)]
        value = value + lax.ppermute(value, axis, pairs)
        reach *= 2
    return value


def product_kernel(left, right, out):
    out[...] = exact(left[...], right[...])


def product(left, right):
    (rows, depth), cols = left.shape, right.shape[1]
    tall, wide = min(128, rows), min(128, cols)
    return pl.pallas_call(
        product_kernel,
        grid=(rows // tall, cols // wide),
        in_specs=[
            pl.BlockSpec((tall, depth), lambda i, j: (i, 0)),
            pl.BlockSpec((depth, wide), lambda i, j: (0, j)),
        ],
        out_specs=pl.BlockSpec((tall, wide), lambda i, j: (i, j)),
        out_shape=jax.ShapeDtypeStruct((rows, cols), jnp.float32),
    )(left, right)


def newton(matrix):
    unit = jnp.eye(matrix.shape[0], dtype=jnp.float32)

    def more(state):
        index, _, norm = state
        return (index < 60) & jnp.logical_not(norm < 1e-7)

    def step(state):
        index, inverse, _ = state
        error = unit - product(matrix, inverse)
        return index + 1, inverse + product(inverse, error), jnp.sum(error * error)

    inverse = unit / jnp.max(jnp.sum(jnp.abs(matrix), axis=0))
    return lax.while_loop(more, step, (jnp.int32(0), inverse, jnp.float32(1.0)))[1]


def crowded(prior, prepared, row_sites, col_sites, error_var, row_place, col_place):
    rows, cols = prior.shape
    row_first = lax.axis_index("row") * rows
    col_first = lax.axis_index("col") * cols
    k = error_var.shape[1]
    chooser = one_hot(col_sites - col_first, cols)
    field, picked = transport(prior, prepared, chooser, 1)
    row_part = pick_rows(field, row_sites, row_first)
    crossing = product(row_part, chooser.astype(jnp.float32).T)
    crossing = added_up(added_up(crossing, "row"), "col")
    row_panel = added_up(row_part, "row")
    column_panel = added_up(picked, "col")

    def body(b, state):
        crossing, row_panel, column_panel, field = state
        mine = b * k
        block = lax.dynamic_slice(crossing, (mine, mine), (k, k))
        variance = lax.dynamic_index_in_dim(error_var, b, 0, keepdims=False)
        inverse = newton(jnp.diag(variance) + product(block, block.T))
        picked_rows = lax.dynamic_slice_in_dim(row_panel, mine, k, axis=0)
        picked_cols = lax.dynamic_slice_in_dim(column_panel, mine, k, axis=0).T
        weights = product(inverse, picked_rows)
        field = field - product(picked_cols, weights)
        cross_rows = lax.dynamic_slice_in_dim(crossing, mine, k, axis=0)
        cross_cols = lax.dynamic_slice_in_dim(crossing, mine, k, axis=1)
        row_panel = row_panel - product(cross_cols, weights)
        gains = product(inverse, cross_rows)
        column_panel = column_panel - product(gains.T, picked_cols.T)
        return crossing - product(cross_cols, gains), row_panel, column_panel, field

    state = (crossing, row_panel, column_panel, field)
    return lax.fori_loop(0, error_var.shape[0], body, state)[3]


def shards(
    prior,
    ozone_courant,
    ozone_diffusion,
    ozone_wind,
    carbon_courant,
    carbon_diffusion,
    carbon_wind,
    ozone_sites,
    carbon_sites,
    error_var,
):
    rows, cols = prior.shape
    row_sites = ozone_sites.reshape(-1)
    col_sites = carbon_sites.reshape(-1)
    ozone = (ozone_courant, ozone_diffusion, ozone_wind)
    carbon = (carbon_courant, carbon_diffusion, carbon_wind)
    row_place = places(row_sites, rows)
    col_place = places(col_sites, cols)
    total = row_sites.size
    fits = (jnp.max(row_place[1]) < capacity(total, lax.axis_size("row"))) & (
        jnp.max(col_place[1]) < capacity(total, lax.axis_size("col"))
    )
    prepared = surroundings(
        prior, ozone, carbon, lax.axis_index("row") * rows, lax.axis_index("col") * cols
    )
    given = (prior, prepared, row_sites, col_sites, error_var, row_place, col_place)
    return lax.cond(fits, balanced, crowded, *given)


def solution(mesh):
    placed = (P("row", "col"), P(), P(), P(), P(), P(), P(), P(), P(), P())
    return jax.shard_map(
        shards, mesh=mesh, in_specs=placed, out_specs=P("row", "col"), check_vma=False
    )
```

```python
import math
import jax
import jax.numpy as jnp
from jax import lax
from jax.experimental import pallas as pl
from jax.experimental.pallas import tpu as pltpu
from jax.sharding import PartitionSpec as P

STEPS = 2
MARGIN = 8
LANES = 128
TILE = 128
HIGHEST = lax.Precision.HIGHEST
LAST = 4
SCALE = 1.5


def coefficients(courant, diffusion, wind, first_cell, before, after, count):
    pad = (before, after)
    total = count + before + after

    def cut(values):
        return lax.dynamic_slice_in_dim(jnp.pad(values, pad), first_cell, total)

    c, d, w = cut(courant), cut(diffusion), cut(wind)
    low = d + jnp.where(w == 0, c, 0.0)
    high = d + jnp.where(w == 0, 0.0, c)
    return low, 1.0 - c - 2.0 * d, high


def edges(value, axis, dim, width):
    size, length = lax.axis_size(axis), value.shape[dim]
    up = [(i, i + 1) for i in range(size - 1)]
    down = [(i + 1, i) for i in range(size - 1)]
    last = lax.slice_in_dim(value, length - width, length, axis=dim)
    leading = lax.slice_in_dim(value, 0, width, axis=dim)
    return lax.ppermute(last, axis, up), lax.ppermute(leading, axis, down)


def across(left, right):
    return lax.dot_general(
        left, right, (((1,), (1,)), ((), ())), preferred_element_type=jnp.float32
    )


def transport_kernel(main, prev, follow, above, below, side, row_weights, col_weights, chooser, out, *picked):
    step = pl.program_id(0)
    last = pl.num_programs(0) - 1
    top = jnp.where(step == 0, above[...], prev[...])
    bottom = jnp.where(step == last, below[...], follow[...])
    body = jnp.concatenate([top, main[...], bottom], axis=0)
    value = jnp.concatenate([body, side[0]], axis=1)
    weights = row_weights[0]
    low, mid, high = weights[:, 0:1], weights[:, 1:2], weights[:, 2:3]
    rows = value.shape[0]
    for _ in range(STEPS):
        value = low * pltpu.roll(value, 1, 0) + mid * value + high * pltpu.roll(value, rows - 1, 0)
    value = value[MARGIN : rows - MARGIN]
    width = value.shape[1]
    low, mid, high = col_weights[0:1], col_weights[1:2], col_weights[2:3]
    for _ in range(STEPS):
        value = low * pltpu.roll(value, 1, 1) + mid * value + high * pltpu.roll(value, width - 1, 1)
    value = value[:, : out.shape[1]]
    out[...] = value
    coarse = value.astype(jnp.bfloat16)
    fine = (value - coarse.astype(jnp.float32)).astype(jnp.bfloat16)
    chosen = across(chooser[...], coarse) + across(chooser[...], fine)
    count = chosen.shape[0] // len(picked)
    for index, part in enumerate(picked):
        part[...] = chosen[index * count : (index + 1) * count]


def surroundings(prior, ozone, carbon, row_first, col_first):
    rows, cols = prior.shape
    tiles, per = rows // TILE, TILE // MARGIN
    above, below = edges(prior, "row", 0, MARGIN)
    left, right = edges(prior, "col", 1, STEPS)
    strips = jnp.concatenate([right, left], axis=1)
    strip_above, strip_below = edges(strips, "row", 0, MARGIN)
    strips = jnp.concatenate([strip_above, strips, strip_below], axis=0)
    strips = jnp.concatenate(
        [
            strips[:, :STEPS],
            jnp.zeros((strips.shape[0], LANES - 2 * STEPS), jnp.float32),
            strips[:, STEPS:],
        ],
        axis=1,
    )

    def windows(values):
        parts = values.reshape((tiles * per + 2, MARGIN) + values.shape[1:])
        main = parts[: tiles * per].reshape((tiles, TILE) + values.shape[1:])
        tail = parts[per:].reshape((-1,) + values.shape[1:])
        tail = jnp.stack([tail[i * TILE : i * TILE + 2 * MARGIN] for i in range(tiles)])
        return jnp.concatenate([main, tail], axis=1)

    side = windows(strips)
    row_weights = windows(
        jnp.stack(coefficients(*ozone, row_first, MARGIN, MARGIN, rows), axis=1)
    )
    row_weights = jnp.pad(row_weights, ((0, 0), (0, 0), (0, 5)))
    trio = coefficients(*carbon, col_first, STEPS, STEPS, cols)
    rolled = []
    for entry in trio:
        filler = jnp.zeros((LANES - 2 * STEPS,), jnp.float32)
        rolled.append(jnp.concatenate([entry[STEPS:], filler, entry[:STEPS]]))
    col_weights = jnp.pad(jnp.stack(rolled), ((0, 5), (0, 0)))
    return above, below, side, row_weights, col_weights


def transport(prior, prepared, chooser, pieces):
    rows, cols = prior.shape
    tiles, per = rows // TILE, TILE // MARGIN
    extent = TILE + 2 * MARGIN
    count = chooser.shape[0] // pieces
    blocks = rows // MARGIN
    return pl.pallas_call(
        transport_kernel,
        grid=(tiles,),
        in_specs=[
            pl.BlockSpec((TILE, cols), lambda i: (i, 0)),
            pl.BlockSpec((MARGIN, cols), lambda i: (jnp.maximum(i * per - 1, 0), 0)),
            pl.BlockSpec((MARGIN, cols), lambda i: (jnp.minimum((i + 1) * per, blocks - 1), 0)),
            pl.BlockSpec((MARGIN, cols), lambda i: (0, 0)),
            pl.BlockSpec((MARGIN, cols), lambda i: (0, 0)),
            pl.BlockSpec((1, extent, LANES), lambda i: (i, 0, 0)),
            pl.BlockSpec((1, extent, 8), lambda i: (i, 0, 0)),
            pl.BlockSpec((8, cols + LANES), lambda i: (0, 0)),
            pl.BlockSpec(chooser.shape, lambda i: (0, 0)),
        ],
        out_specs=[
            pl.BlockSpec((TILE, cols), lambda i: (i, 0)),
        ]
        + [pl.BlockSpec((count, TILE), lambda i: (0, i))] * pieces,
        out_shape=[
            jax.ShapeDtypeStruct((rows, cols), jnp.float32),
        ]
        + [jax.ShapeDtypeStruct((count, rows), jnp.float32)] * pieces,
        compiler_params=pltpu.CompilerParams(vmem_limit_bytes=60 << 20),
    )(prior, prior, prior, *prepared, chooser)


def plain(first_matrix, second_matrix):
    return jnp.dot(first_matrix, second_matrix, preferred_element_type=jnp.float32)


def exact(first_matrix, second_matrix):
    return jnp.dot(
        first_matrix, second_matrix, precision=HIGHEST, preferred_element_type=jnp.float32
    )


def halves(value):
    coarse = value.astype(jnp.bfloat16)
    return coarse, (value - coarse.astype(jnp.float32)).astype(jnp.bfloat16)


def by_rows(count, step, write):
    def body(index, carry):
        write(pl.ds(pl.multiple_of(index * step, step), step))
        return carry

    lax.fori_loop(0, count // step, body, 0)


def chunk(count):
    return next(n for n in (512, 640, 256, 128, 16) if count % n == 0)


def below(rows, first):
    return pl.ds(rows.start + first, rows.size)


def unit_rows(rows, k):
    down = lax.broadcasted_iota(jnp.int32, (rows.size, k), 0) + rows.start
    return (down == lax.broadcasted_iota(jnp.int32, (rows.size, k), 1)).astype(jnp.float32)


def cut(parts, value, rows=slice(None)):
    for index in range(parts.shape[0]):
        term = value.astype(jnp.bfloat16)
        parts[index, rows, :] = term
        value = value - term.astype(jnp.float32)


def joined(left, right, rows, product=plain):
    small = product(left[0, rows, :], right[2]) + product(left[2, rows, :], right[0])
    small += product(left[1, rows, :], right[1])
    small += product(left[0, rows, :], right[1]) + product(left[1, rows, :], right[0])
    return small + product(left[0, rows, :], right[0])


def whole_call(kernel, outs, scratch, *args, cost):
    whole = pl.BlockSpec(memory_space=pltpu.VMEM)
    return pl.pallas_call(
        kernel,
        in_specs=[whole] * len(args),
        out_specs=[whole] * len(outs),
        out_shape=[jax.ShapeDtypeStruct(*out) for out in outs],
        scratch_shapes=[pltpu.VMEM(*entry) for entry in scratch],
        cost_estimate=pl.CostEstimate(
            flops=int(cost * SCALE * 1e9), bytes_accessed=1 << 20, transcendentals=0
        ),
        compiler_params=pltpu.CompilerParams(vmem_limit_bytes=60 << 20),
    )(*args)


def assemble_kernel(slotted, place, g, parts):
    cut(parts, slotted[...])

    def write(rows):
        picks = place[rows, :]
        g[rows, :] = plain(picks, parts[0]) + plain(picks, parts[1]) + plain(picks, parts[2])

    by_rows(g.shape[0], chunk(g.shape[0]), write)
    g[...] = g[...].T


def invert_kernel(block, variance, x, s, sp, xp, ep):
    k = s.shape[0]
    step = chunk(k)
    cut(xp, block[...])

    def innovation(rows):
        s[rows, :] = unit_rows(rows, k) * variance[...] + joined(xp, xp, rows, across)

    by_rows(k, step, innovation)
    cut(sp, s[...])
    bound = jnp.max(jnp.sum(jnp.abs(s[...]), axis=0))

    def begin():
        x[...] = (1.0 / bound) * unit_rows(pl.ds(0, k), k)
        cut(xp, x[...])

    def residual(precise):
        def body(index, total):
            rows = pl.ds(pl.multiple_of(index * step, step), step)
            if precise:
                left = unit_rows(rows, k) - joined(sp, xp, rows)
                cut(ep, left, rows)
            else:
                left = unit_rows(rows, k) - plain(sp[0, rows, :], xp[0])
                ep[0, rows, :] = left.astype(jnp.bfloat16)
            return total + jnp.sum(left * left)

        return lax.fori_loop(0, k // step, body, jnp.float32(0.0))

    def improve(precise):
        def write(rows):
            value = plain(xp[0, rows, :], ep[0])
            if precise:
                value += plain(xp[0, rows, :], ep[1]) + plain(xp[1, rows, :], ep[0])
            value += x[rows, :]
            x[rows, :] = value
            if precise:
                cut(xp, value, rows)
            else:
                xp[0, rows, :] = value.astype(jnp.bfloat16)

        by_rows(k, step, write)

    begin()
    first = residual(False)

    def coarse_more(state):
        index, norm = state
        return (index < 14) & (norm > 0.25) & (norm <= 1.1 * first)

    def coarse_step(state):
        index, _ = state
        improve(False)
        return index + 1, residual(False)

    lax.while_loop(coarse_more, coarse_step, (jnp.int32(0), first))
    cut(xp, x[...])

    def fine_more(state):
        index, norm = state
        return (index < 60) & jnp.logical_not(norm < 1e-5)

    def fine_step(state):
        index, norm = state

        @pl.when((index == 0) | (norm < 0.8) | (index > 1))
        def _():
            @pl.when(index > 0)
            def _():
                improve(True)

        @pl.when((index == 1) & jnp.logical_not(norm < 0.8))
        def _():
            begin()

        return index + 1, residual(True)

    lax.while_loop(fine_more, fine_step, (jnp.int32(0), jnp.float32(1.0)))
    improve(True)


def deflate_kernel(g, x0, carry, block, left, right):
    k = x0.shape[0]
    step = chunk(k)
    cut(left, g[k:, :k])
    cut(right, x0[...])

    def carry_rows(rows):
        carry[rows, :] = joined(left, right, rows)

    by_rows(k, step, carry_rows)
    cut(left, carry[...])
    cut(right, g[:k, k:])

    def block_rows(rows):
        block[rows, :] = g[below(rows, k), k:] - joined(left, right, rows)

    by_rows(k, step, block_rows)


def gain_kernel(g, x0, x1, carry, spots, back, coarse_out, fine_out, hp, ap, xp, tp, part):
    k = x0.shape[0]
    step = chunk(k)
    low, high = pl.ds(0, k), pl.ds(k, k)

    def put(rows, columns, value):
        coarse, fine = halves(value)
        part[0, rows, columns] = coarse
        part[1, rows, columns] = fine

    cut(hp, x0[...])
    cut(ap, g[:k, k:])

    def h_rows(rows):
        cut(xp, joined(hp, ap, rows), rows)

    by_rows(k, step, h_rows)
    for index in range(3):
        hp[index] = xp[index]
    cut(xp, x1[...])

    def right_rows(rows):
        put(rows, high, -joined(hp, xp, rows))
        put(below(rows, k), high, x1[rows, :])

    by_rows(k, step, right_rows)

    def a_rows(rows):
        value = joined(xp, ap, rows)
        put(below(rows, k), low, -value)
        cut(tp, value, rows)

    cut(ap, carry[...])
    by_rows(k, step, a_rows)

    def left_rows(rows):
        put(rows, low, x0[rows, :] + joined(hp, tp, rows))

    by_rows(k, step, left_rows)

    def slot_rows(rows):
        picks = back[rows, :]
        for index, out in ((0, coarse_out), (1, fine_out)):
            moved = plain(picks, part[index]).astype(jnp.bfloat16)
            out[rows, :] = plain(moved, spots[...]).astype(jnp.bfloat16)

    by_rows(back.shape[0], chunk(back.shape[0]), slot_rows)


def gain(slotted, place, spots, back, variance):
    slots, both = slotted.shape
    k = both // 2
    square = ((k, k), jnp.float32)
    terms = ((3, k, k), jnp.bfloat16)
    (g,) = whole_call(
        assemble_kernel,
        [((both, both), jnp.float32)],
        [((3, slots, both), jnp.bfloat16)],
        slotted,
        place,
        cost=17,
    )

    def inverse(block, b):
        scratch = [square, terms, terms, terms]
        return whole_call(
            invert_kernel, [square], scratch, block, variance[b : b + 1], cost=21
        )[0]

    x0 = inverse(g[:k, :k], 0)
    carry, block = whole_call(deflate_kernel, [square, square], [terms, terms], g, x0, cost=7)
    x1 = inverse(block, 1)
    out = ((slots, spots.shape[1]), jnp.bfloat16)
    return whole_call(
        gain_kernel,
        [out, out],
        [terms] * 4 + [((2, both, both), jnp.bfloat16)],
        g,
        x0,
        x1,
        carry,
        spots,
        back,
        cost=26,
    )


def crossing_kernel(known, slotted, send, recv, side_send, side_recv):
    size = lax.axis_size("col")
    half, side = known.shape[0] // 2, known.shape[1] // 2
    row, col = lax.axis_index("row"), lax.axis_index("col")
    core = row % 2
    even = col % 2 == 0
    ahead = jnp.where(
        even,
        jnp.where(col + 2 < size, col + 2, col + 1),
        jnp.where(col > 1, col - 2, col - 1),
    )
    behind = jnp.where(
        even,
        jnp.where(col > 1, col - 2, col + 1),
        jnp.where(col + 2 < size, col + 2, col - 1),
    )
    partner = row + 1 - 2 * core
    mesh_ids = pl.DeviceIdType.MESH
    barrier = pltpu.get_barrier_semaphore()
    for device in ({"col": ahead}, {"col": behind}, {"row": partner}):
        pl.semaphore_signal(barrier, inc=1, device_id=device, device_id_type=mesh_ids)
    pl.semaphore_wait(barrier, 3)
    columns = pl.ds(pl.multiple_of(core * side, side), side)

    def slot(way, step):
        return slotted.at[pl.ds((2 * step + way) * half, half), columns]

    def source(way, step):
        if step == 0:
            return known.at[pl.ds(way * half, half), columns]
        return slot(way, step)

    copies, sides = {}, []
    for step in range(size):
        for way, device in ((0, {"col": ahead}), (1, {"col": behind})):
            if step:
                copies[way, step - 1].wait_recv()
            if step < size - 1:
                copy = pltpu.make_async_remote_copy(
                    src_ref=source(way, step),
                    dst_ref=slot(way, step + 1),
                    send_sem=send.at[way, step],
                    recv_sem=recv.at[way, step],
                    device_id=device,
                    device_id_type=mesh_ids,
                )
                copy.start()
                copies[way, step] = copy
            copy = pltpu.make_async_remote_copy(
                src_ref=source(way, step),
                dst_ref=slot(way, step),
                send_sem=side_send.at[way, step],
                recv_sem=side_recv.at[way, step],
                device_id={"row": partner},
                device_id_type=mesh_ids,
            )
            copy.start()
            sides.append(copy)
            if step == 0:
                slotted[pl.ds(way * half, half), columns] = known[
                    pl.ds(way * half, half), columns
                ]
    for copy in copies.values():
        copy.wait_send()
    for copy in sides:
        copy.wait()


def crossing_gather(known):
    size = lax.axis_size("col")
    whole = pl.BlockSpec(memory_space=pltpu.VMEM)
    sems = pltpu.SemaphoreType.DMA((2, size))
    return pl.pallas_call(
        crossing_kernel,
        in_specs=[whole],
        out_specs=whole,
        out_shape=jax.ShapeDtypeStruct((known.shape[0] * size, known.shape[1]), known.dtype),
        scratch_shapes=[sems] * 4,
        compiler_params=pltpu.CompilerParams(collective_id=0, has_side_effects=True),
    )(known)


def weights_kernel(gain_coarse, gain_fine, *refs):
    panels, (coarse_out, fine_out) = refs[:-2], refs[-2:]
    coarse, fine = halves(jnp.concatenate([panel[...] for panel in panels], axis=0))

    def write(rows):
        value = plain(gain_coarse[rows, :], coarse)
        value += plain(gain_coarse[rows, :], fine) + plain(gain_fine[rows, :], coarse)
        coarse_out[rows, :], fine_out[rows, :] = halves(value)

    by_rows(gain_coarse.shape[0], gain_coarse.shape[0], write)


def weights_of(gain_coarse, gain_fine, panels):
    slots = gain_coarse.shape[0]
    cols = panels[0].shape[1]
    wide = min(256, cols)
    held = pl.BlockSpec(gain_coarse.shape, lambda j: (0, 0), pipeline_mode=pl.Buffered(1))
    out = jax.ShapeDtypeStruct((slots, cols), jnp.bfloat16)
    return pl.pallas_call(
        weights_kernel,
        grid=(cols // wide,),
        in_specs=[held, held]
        + [pl.BlockSpec((p.shape[0], wide), lambda j: (0, j)) for p in panels],
        out_specs=[pl.BlockSpec((slots, wide), lambda j: (0, j))] * 2,
        out_shape=[out, out],
        cost_estimate=pl.CostEstimate(
            flops=6 * slots * gain_coarse.shape[1] * cols,
            bytes_accessed=12 * slots * cols,
            transcendentals=0,
        ),
        compiler_params=pltpu.CompilerParams(vmem_limit_bytes=60 << 20),
    )(gain_coarse, gain_fine, *panels)


def update_kernel(field, weights_coarse, weights_fine, *refs):
    panels, out = refs[:-1], refs[-1]
    panel = jnp.concatenate([part[...] for part in panels], axis=0).T
    coarse, fine = halves(panel)
    wide = min(512, out.shape[1])

    for index in range(out.shape[1] // wide):
        columns = pl.ds(index * wide, wide)
        value = plain(coarse, weights_coarse[:, columns])
        value += plain(coarse, weights_fine[:, columns])
        value += plain(fine, weights_coarse[:, columns])
        out[:, columns] = field[:, columns] - value


def update(field, weights_coarse, weights_fine, panels, piece):
    rows, cols = field.shape
    tall = min(256, rows)
    tile = pl.BlockSpec((tall, cols), lambda i: (i, 0))
    slots = len(panels) * panels[0].shape[0]
    held = pl.BlockSpec((slots, cols), lambda i: (piece, 0), pipeline_mode=pl.Buffered(1))
    return pl.pallas_call(
        update_kernel,
        grid=(rows // tall,),
        in_specs=[tile, held, held]
        + [pl.BlockSpec((p.shape[0], tall), lambda i: (0, i)) for p in panels],
        out_specs=tile,
        out_shape=jax.ShapeDtypeStruct(field.shape, jnp.float32),
        cost_estimate=pl.CostEstimate(
            flops=8 * slots * rows * cols, bytes_accessed=8 * rows * cols, transcendentals=0
        ),
        compiler_params=pltpu.CompilerParams(vmem_limit_bytes=60 << 20),
    )(field, weights_coarse, weights_fine, *panels)


def capacity(total, parts):
    mean = total / parts
    need = math.ceil((mean + 3.0 * math.sqrt(mean * (1 - 1 / parts))) / 16) * 16
    return min(need, total)


def ring_of(size):
    return list(range(0, size, 2)) + list(range(size - 1 - size % 2, 0, -2))


def ring_gather(up_part, down_part, axis, after):
    cycle = ring_of(lax.axis_size(axis))
    ahead = [(cycle[i], cycle[(i + 1) % len(cycle)]) for i in range(len(cycle))]
    behind = [(b, a) for a, b in ahead]
    ups, downs = [up_part], [down_part]
    for _ in range(1, len(cycle)):
        ups.append(lax.ppermute(ups[-1], axis, ahead))
        downs.append(lax.ppermute(downs[-1], axis, behind))
        if len(ups) == 2:
            ups[1], downs[1], after = lax.optimization_barrier((ups[1], downs[1], after))
    return [part for pair in zip(ups, downs) for part in pair], after


def doubling_masks(size):
    masks, reach = [0], size // 2
    while reach:
        masks += [mask ^ reach for mask in masks]
        reach //= 2
    return masks


def doubling_gather(value, axis):
    size = lax.axis_size(axis)
    parts, reach = [value], size // 2
    while reach:
        pairs = [(i, i ^ reach) for i in range(size)]
        parts += [lax.ppermute(part, axis, pairs) for part in parts]
        reach //= 2
    return parts


def lookup(table, index):
    return jnp.sum(
        jnp.where(index[:, None] == jnp.arange(len(table))[None, :], jnp.array(table)[None, :], 0),
        axis=1,
    )


def places(sites, extent):
    owner = sites // extent
    before = jnp.tril(jnp.ones((sites.size, sites.size), jnp.bool_), -1)
    same = owner[:, None] == owner[None, :]
    return owner, jnp.sum((same & before).astype(jnp.int32), axis=1)


def local_cells(sites, owner, rank, me, extent, count, empty):
    hit = (owner == me)[None, :] & (rank[None, :] == jnp.arange(count)[:, None])
    cell = jnp.sum(jnp.where(hit, (sites - me * extent - empty)[None, :], 0), axis=1)
    return cell + empty


def one_hot(index, count):
    return (index[:, None] == jnp.arange(count)[None, :]).astype(jnp.bfloat16)


def pick_rows(matrix, sites, first_cell):
    count = matrix.shape[0]
    offsets = sites - first_cell
    owned = (offsets >= 0) & (offsets < count)
    picked = matrix[jnp.clip(offsets, 0, count - 1)]
    return jnp.where(owned[:, None], picked, 0.0)


def pick_kernel(cells, chooser, field, picked, crossing, groups, sem):
    count = picked.shape[0]

    def fetch(index, carry):
        group = pl.multiple_of(cells[index] // MARGIN * MARGIN, MARGIN)
        spot = pl.multiple_of(index * MARGIN, MARGIN)
        pltpu.make_async_copy(
            field.at[pl.ds(group, MARGIN)], groups.at[pl.ds(spot, MARGIN)], sem
        ).start()
        return carry

    lax.fori_loop(0, count, fetch, 0)
    pltpu.make_async_copy(groups, groups, sem).wait()

    def settle(index, carry):
        spot = index * MARGIN + lax.rem(cells[index], MARGIN)
        picked[pl.ds(index, 1), :] = groups[pl.ds(spot, 1), :]
        return carry

    lax.fori_loop(0, count, settle, 0, unroll=8)
    value = picked[...]
    total = jnp.zeros(crossing.shape, jnp.float32)
    for _ in range(3):
        term = value.astype(jnp.bfloat16)
        total += across(chooser[...], term)
        value = value - term.astype(jnp.float32)
    crossing[...] = total


def pick(field, cells, chooser):
    count, cols = cells.size, field.shape[1]
    held = pl.BlockSpec(memory_space=pltpu.VMEM)
    return pl.pallas_call(
        pick_kernel,
        in_specs=[
            pl.BlockSpec(memory_space=pltpu.SMEM),
            held,
            pl.BlockSpec(memory_space=pl.ANY),
        ],
        out_specs=[held, held],
        out_shape=[
            jax.ShapeDtypeStruct((count, cols), jnp.float32),
            jax.ShapeDtypeStruct((chooser.shape[0], count), jnp.float32),
        ],
        scratch_shapes=[
            pltpu.VMEM((count * MARGIN, cols), jnp.float32),
            pltpu.SemaphoreType.DMA,
        ],
        cost_estimate=pl.CostEstimate(
            flops=40 * 10**9, bytes_accessed=1 << 20, transcendentals=0
        ),
        compiler_params=pltpu.CompilerParams(vmem_limit_bytes=60 << 20),
    )(cells, chooser, field)


def balanced(prior, prepared, row_sites, col_sites, error_var, row_place, col_place):
    rows, cols = prior.shape
    across_rows, across_cols = lax.axis_size("row"), lax.axis_size("col")
    my_row, my_col = lax.axis_index("row"), lax.axis_index("col")
    total = row_sites.size
    row_slots, col_slots = capacity(total, across_rows), capacity(total, across_cols)
    row_owner, row_rank = row_place
    col_owner, col_rank = col_place
    half = col_slots // 2

    my_rows = local_cells(row_sites, row_owner, row_rank, my_row, rows, row_slots, 0)
    my_cols = local_cells(col_sites, col_owner, col_rank, my_col, cols, col_slots, -1)
    chooser = one_hot(my_cols, cols)

    masks = doubling_masks(across_rows)
    order = [masks.index(mask) for mask in range(across_rows)]
    row_slot = lookup(order, row_owner ^ my_row) * row_slots + row_rank
    cycle = ring_of(across_cols)
    spot = [cycle.index(c) for c in range(across_cols)]
    here = lookup(spot, my_col[None])[0]
    away = lookup(spot, col_owner) - here
    up_step, down_step = (-away) % across_cols, away % across_cols
    col_slot = jnp.where(
        col_rank < half,
        2 * up_step * half + col_rank,
        2 * down_step * half + col_rank,
    )
    spots = one_hot(row_slot, across_rows * row_slots)
    place = one_hot(col_slot, across_cols * col_slots)

    field, up_part, down_part = transport(prior, prepared, chooser, 2)
    row_part, crossing = pick(field, my_rows, chooser)
    pieces = doubling_gather(crossing, "row")
    known = exact(jnp.concatenate(pieces, axis=1), spots.astype(jnp.float32).T)
    row_part, known = lax.optimization_barrier((row_part, known))
    slotted = crossing_gather(known)
    panels = doubling_gather(row_part, "row")
    parts, slotted = ring_gather(up_part, down_part, "col", slotted)
    gain_coarse, gain_fine = gain(slotted, place, spots, place.T, error_var)
    weights = weights_of(gain_coarse, gain_fine, panels)
    last = len(parts) // LAST
    field = update(field, *weights, parts[:-last], 0)
    return update(field, *weights, parts[-last:], LAST - 1)


def added_up(value, axis):
    size, reach = lax.axis_size(axis), 1
    while reach < size:
        pairs = [(i, i ^ reach) for i in range(size)]
        value = value + lax.ppermute(value, axis, pairs)
        reach *= 2
    return value


def product_kernel(left, right, out):
    out[...] = exact(left[...], right[...])


def product(left, right):
    (rows, depth), cols = left.shape, right.shape[1]
    tall, wide = min(128, rows), min(128, cols)
    return pl.pallas_call(
        product_kernel,
        grid=(rows // tall, cols // wide),
        in_specs=[
            pl.BlockSpec((tall, depth), lambda i, j: (i, 0)),
            pl.BlockSpec((depth, wide), lambda i, j: (0, j)),
        ],
        out_specs=pl.BlockSpec((tall, wide), lambda i, j: (i, j)),
        out_shape=jax.ShapeDtypeStruct((rows, cols), jnp.float32),
    )(left, right)


def newton(matrix):
    unit = jnp.eye(matrix.shape[0], dtype=jnp.float32)

    def more(state):
        index, _, norm = state
        return (index < 60) & jnp.logical_not(norm < 1e-7)

    def step(state):
        index, inverse, _ = state
        error = unit - product(matrix, inverse)
        return index + 1, inverse + product(inverse, error), jnp.sum(error * error)

    inverse = unit / jnp.max(jnp.sum(jnp.abs(matrix), axis=0))
    return lax.while_loop(more, step, (jnp.int32(0), inverse, jnp.float32(1.0)))[1]


def crowded(prior, prepared, row_sites, col_sites, error_var, row_place, col_place):
    rows, cols = prior.shape
    row_first = lax.axis_index("row") * rows
    col_first = lax.axis_index("col") * cols
    k = error_var.shape[1]
    chooser = one_hot(col_sites - col_first, cols)
    field, picked = transport(prior, prepared, chooser, 1)
    row_part = pick_rows(field, row_sites, row_first)
    crossing = product(row_part, chooser.astype(jnp.float32).T)
    crossing = added_up(added_up(crossing, "row"), "col")
    row_panel = added_up(row_part, "row")
    column_panel = added_up(picked, "col")

    def body(b, state):
        crossing, row_panel, column_panel, field = state
        mine = b * k
        block = lax.dynamic_slice(crossing, (mine, mine), (k, k))
        variance = lax.dynamic_index_in_dim(error_var, b, 0, keepdims=False)
        inverse = newton(jnp.diag(variance) + product(block, block.T))
        picked_rows = lax.dynamic_slice_in_dim(row_panel, mine, k, axis=0)
        picked_cols = lax.dynamic_slice_in_dim(column_panel, mine, k, axis=0).T
        weights = product(inverse, picked_rows)
        field = field - product(picked_cols, weights)
        cross_rows = lax.dynamic_slice_in_dim(crossing, mine, k, axis=0)
        cross_cols = lax.dynamic_slice_in_dim(crossing, mine, k, axis=1)
        row_panel = row_panel - product(cross_cols, weights)
        gains = product(inverse, cross_rows)
        column_panel = column_panel - product(gains.T, picked_cols.T)
        return crossing - product(cross_cols, gains), row_panel, column_panel, field

    state = (crossing, row_panel, column_panel, field)
    return lax.fori_loop(0, error_var.shape[0], body, state)[3]


def shards(
    prior,
    ozone_courant,
    ozone_diffusion,
    ozone_wind,
    carbon_courant,
    carbon_diffusion,
    carbon_wind,
    ozone_sites,
    carbon_sites,
    error_var,
):
    rows, cols = prior.shape
    row_sites = ozone_sites.reshape(-1)
    col_sites = carbon_sites.reshape(-1)
    ozone = (ozone_courant, ozone_diffusion, ozone_wind)
    carbon = (carbon_courant, carbon_diffusion, carbon_wind)
    row_place = places(row_sites, rows)
    col_place = places(col_sites, cols)
    total = row_sites.size
    fits = (jnp.max(row_place[1]) < capacity(total, lax.axis_size("row"))) & (
        jnp.max(col_place[1]) < capacity(total, lax.axis_size("col"))
    )
    prepared = surroundings(
        prior, ozone, carbon, lax.axis_index("row") * rows, lax.axis_index("col") * cols
    )
    given = (prior, prepared, row_sites, col_sites, error_var, row_place, col_place)
    return lax.cond(fits, balanced, crowded, *given)


def solution(mesh):
    placed = (P("row", "col"), P(), P(), P(), P(), P(), P(), P(), P(), P())
    return jax.shard_map(
        shards, mesh=mesh, in_specs=placed, out_specs=P("row", "col"), check_vma=False
    )
```

```python
import math
import jax
import jax.numpy as jnp
from jax import lax
from jax.experimental import pallas as pl
from jax.experimental.pallas import tpu as pltpu
from jax.sharding import PartitionSpec as P

STEPS = 2
MARGIN = 8
LANES = 128
TILE = 128
HIGHEST = lax.Precision.HIGHEST
LAST = 4
SCALE = 1.5


def coefficients(courant, diffusion, wind, first_cell, before, after, count):
    pad = (before, after)
    total = count + before + after

    def cut(values):
        return lax.dynamic_slice_in_dim(jnp.pad(values, pad), first_cell, total)

    c, d, w = cut(courant), cut(diffusion), cut(wind)
    low = d + jnp.where(w == 0, c, 0.0)
    high = d + jnp.where(w == 0, 0.0, c)
    return low, 1.0 - c - 2.0 * d, high


def edges(value, axis, dim, width):
    size, length = lax.axis_size(axis), value.shape[dim]
    up = [(i, i + 1) for i in range(size - 1)]
    down = [(i + 1, i) for i in range(size - 1)]
    last = lax.slice_in_dim(value, length - width, length, axis=dim)
    leading = lax.slice_in_dim(value, 0, width, axis=dim)
    return lax.ppermute(last, axis, up), lax.ppermute(leading, axis, down)


def across(left, right):
    return lax.dot_general(
        left, right, (((1,), (1,)), ((), ())), preferred_element_type=jnp.float32
    )


def transport_kernel(main, prev, follow, above, below, side, row_weights, col_weights, chooser, out, *picked):
    step = pl.program_id(0)
    last = pl.num_programs(0) - 1
    top = jnp.where(step == 0, above[...], prev[...])
    bottom = jnp.where(step == last, below[...], follow[...])
    body = jnp.concatenate([top, main[...], bottom], axis=0)
    value = jnp.concatenate([body, side[0]], axis=1)
    weights = row_weights[0]
    low, mid, high = weights[:, 0:1], weights[:, 1:2], weights[:, 2:3]
    rows = value.shape[0]
    for _ in range(STEPS):
        value = low * pltpu.roll(value, 1, 0) + mid * value + high * pltpu.roll(value, rows - 1, 0)
    value = value[MARGIN : rows - MARGIN]
    width = value.shape[1]
    low, mid, high = col_weights[0:1], col_weights[1:2], col_weights[2:3]
    for _ in range(STEPS):
        value = low * pltpu.roll(value, 1, 1) + mid * value + high * pltpu.roll(value, width - 1, 1)
    value = value[:, : out.shape[1]]
    out[...] = value
    coarse = value.astype(jnp.bfloat16)
    fine = (value - coarse.astype(jnp.float32)).astype(jnp.bfloat16)
    chosen = across(chooser[...], coarse) + across(chooser[...], fine)
    count = chosen.shape[0] // len(picked)
    for index, part in enumerate(picked):
        part[...] = chosen[index * count : (index + 1) * count]


def surroundings(prior, ozone, carbon, row_first, col_first):
    rows, cols = prior.shape
    tiles, per = rows // TILE, TILE // MARGIN
    above, below = edges(prior, "row", 0, MARGIN)
    left, right = edges(prior, "col", 1, STEPS)
    strips = jnp.concatenate([right, left], axis=1)
    strip_above, strip_below = edges(strips, "row", 0, MARGIN)
    strips = jnp.concatenate([strip_above, strips, strip_below], axis=0)
    strips = jnp.concatenate(
        [
            strips[:, :STEPS],
            jnp.zeros((strips.shape[0], LANES - 2 * STEPS), jnp.float32),
            strips[:, STEPS:],
        ],
        axis=1,
    )

    def windows(values):
        parts = values.reshape((tiles * per + 2, MARGIN) + values.shape[1:])
        main = parts[: tiles * per].reshape((tiles, TILE) + values.shape[1:])
        tail = parts[per:].reshape((-1,) + values.shape[1:])
        tail = jnp.stack([tail[i * TILE : i * TILE + 2 * MARGIN] for i in range(tiles)])
        return jnp.concatenate([main, tail], axis=1)

    side = windows(strips)
    row_weights = windows(
        jnp.stack(coefficients(*ozone, row_first, MARGIN, MARGIN, rows), axis=1)
    )
    row_weights = jnp.pad(row_weights, ((0, 0), (0, 0), (0, 5)))
    trio = coefficients(*carbon, col_first, STEPS, STEPS, cols)
    rolled = []
    for entry in trio:
        filler = jnp.zeros((LANES - 2 * STEPS,), jnp.float32)
        rolled.append(jnp.concatenate([entry[STEPS:], filler, entry[:STEPS]]))
    col_weights = jnp.pad(jnp.stack(rolled), ((0, 5), (0, 0)))
    return above, below, side, row_weights, col_weights


def transport(prior, prepared, chooser, pieces):
    rows, cols = prior.shape
    tiles, per = rows // TILE, TILE // MARGIN
    extent = TILE + 2 * MARGIN
    count = chooser.shape[0] // pieces
    blocks = rows // MARGIN
    return pl.pallas_call(
        transport_kernel,
        grid=(tiles,),
        in_specs=[
            pl.BlockSpec((TILE, cols), lambda i: (i, 0)),
            pl.BlockSpec((MARGIN, cols), lambda i: (jnp.maximum(i * per - 1, 0), 0)),
            pl.BlockSpec((MARGIN, cols), lambda i: (jnp.minimum((i + 1) * per, blocks - 1), 0)),
            pl.BlockSpec((MARGIN, cols), lambda i: (0, 0)),
            pl.BlockSpec((MARGIN, cols), lambda i: (0, 0)),
            pl.BlockSpec((1, extent, LANES), lambda i: (i, 0, 0)),
            pl.BlockSpec((1, extent, 8), lambda i: (i, 0, 0)),
            pl.BlockSpec((8, cols + LANES), lambda i: (0, 0)),
            pl.BlockSpec(chooser.shape, lambda i: (0, 0)),
        ],
        out_specs=[
            pl.BlockSpec((TILE, cols), lambda i: (i, 0)),
        ]
        + [pl.BlockSpec((count, TILE), lambda i: (0, i))] * pieces,
        out_shape=[
            jax.ShapeDtypeStruct((rows, cols), jnp.float32),
        ]
        + [jax.ShapeDtypeStruct((count, rows), jnp.float32)] * pieces,
        compiler_params=pltpu.CompilerParams(vmem_limit_bytes=60 << 20),
    )(prior, prior, prior, *prepared, chooser)


def plain(first_matrix, second_matrix):
    return jnp.dot(first_matrix, second_matrix, preferred_element_type=jnp.float32)


def exact(first_matrix, second_matrix):
    return jnp.dot(
        first_matrix, second_matrix, precision=HIGHEST, preferred_element_type=jnp.float32
    )


def halves(value):
    coarse = value.astype(jnp.bfloat16)
    return coarse, (value - coarse.astype(jnp.float32)).astype(jnp.bfloat16)


def by_rows(count, step, write):
    def body(index, carry):
        write(pl.ds(pl.multiple_of(index * step, step), step))
        return carry

    lax.fori_loop(0, count // step, body, 0)


def chunk(count):
    return next(n for n in (512, 640, 256, 128, 16) if count % n == 0)


def below(rows, first):
    return pl.ds(rows.start + first, rows.size)


def unit_rows(rows, k):
    down = lax.broadcasted_iota(jnp.int32, (rows.size, k), 0) + rows.start
    return (down == lax.broadcasted_iota(jnp.int32, (rows.size, k), 1)).astype(jnp.float32)


def cut(parts, value, rows=slice(None)):
    for index in range(parts.shape[0]):
        term = value.astype(jnp.bfloat16)
        parts[index, rows, :] = term
        value = value - term.astype(jnp.float32)


def joined(left, right, rows, product=plain):
    small = product(left[0, rows, :], right[2]) + product(left[2, rows, :], right[0])
    small += product(left[1, rows, :], right[1])
    small += product(left[0, rows, :], right[1]) + product(left[1, rows, :], right[0])
    return small + product(left[0, rows, :], right[0])


def whole_call(kernel, outs, scratch, *args, cost):
    whole = pl.BlockSpec(memory_space=pltpu.VMEM)
    return pl.pallas_call(
        kernel,
        in_specs=[whole] * len(args),
        out_specs=[whole] * len(outs),
        out_shape=[jax.ShapeDtypeStruct(*out) for out in outs],
        scratch_shapes=[pltpu.VMEM(*entry) for entry in scratch],
        cost_estimate=pl.CostEstimate(
            flops=int(cost * SCALE * 1e9), bytes_accessed=1 << 20, transcendentals=0
        ),
        compiler_params=pltpu.CompilerParams(vmem_limit_bytes=60 << 20),
    )(*args)


def assemble_kernel(slotted, place, g, parts):
    cut(parts, slotted[...])

    def write(rows):
        picks = place[rows, :]
        g[rows, :] = plain(picks, parts[0]) + plain(picks, parts[1]) + plain(picks, parts[2])

    by_rows(g.shape[0], chunk(g.shape[0]), write)
    g[...] = g[...].T


def invert_kernel(block, variance, x, s, sp, xp, ep):
    k = s.shape[0]
    step = chunk(k)
    cut(xp, block[...])

    def innovation(rows):
        s[rows, :] = unit_rows(rows, k) * variance[...] + joined(xp, xp, rows, across)

    by_rows(k, step, innovation)
    cut(sp, s[...])
    bound = jnp.max(jnp.sum(jnp.abs(s[...]), axis=0))

    def begin():
        x[...] = (1.0 / bound) * unit_rows(pl.ds(0, k), k)
        cut(xp, x[...])

    def residual(precise):
        def body(index, total):
            rows = pl.ds(pl.multiple_of(index * step, step), step)
            if precise:
                left = unit_rows(rows, k) - joined(sp, xp, rows)
                cut(ep, left, rows)
            else:
                left = unit_rows(rows, k) - plain(sp[0, rows, :], xp[0])
                ep[0, rows, :] = left.astype(jnp.bfloat16)
            return total + jnp.sum(left * left)

        return lax.fori_loop(0, k // step, body, jnp.float32(0.0))

    def improve(precise):
        def write(rows):
            value = plain(xp[0, rows, :], ep[0])
            if precise:
                value += plain(xp[0, rows, :], ep[1]) + plain(xp[1, rows, :], ep[0])
            value += x[rows, :]
            x[rows, :] = value
            if precise:
                cut(xp, value, rows)
            else:
                xp[0, rows, :] = value.astype(jnp.bfloat16)

        by_rows(k, step, write)

    begin()
    first = residual(False)

    def coarse_more(state):
        index, norm = state
        return (index < 14) & (norm > 0.25) & (norm <= 1.1 * first)

    def coarse_step(state):
        index, _ = state
        improve(False)
        return index + 1, residual(False)

    lax.while_loop(coarse_more, coarse_step, (jnp.int32(0), first))
    cut(xp, x[...])

    def fine_more(state):
        index, norm = state
        return (index < 60) & jnp.logical_not(norm < 1e-5)

    def fine_step(state):
        index, norm = state

        @pl.when((index == 0) | (norm < 0.8) | (index > 1))
        def _():
            @pl.when(index > 0)
            def _():
                improve(True)

        @pl.when((index == 1) & jnp.logical_not(norm < 0.8))
        def _():
            begin()

        return index + 1, residual(True)

    lax.while_loop(fine_more, fine_step, (jnp.int32(0), jnp.float32(1.0)))
    improve(True)


def deflate_kernel(g, x0, carry, block, left, right):
    k = x0.shape[0]
    step = chunk(k)
    cut(left, g[k:, :k])
    cut(right, x0[...])

    def carry_rows(rows):
        carry[rows, :] = joined(left, right, rows)

    by_rows(k, step, carry_rows)
    cut(left, carry[...])
    cut(right, g[:k, k:])

    def block_rows(rows):
        block[rows, :] = g[below(rows, k), k:] - joined(left, right, rows)

    by_rows(k, step, block_rows)


def gain_kernel(g, x0, x1, carry, spots, back, coarse_out, fine_out, hp, ap, xp, tp, part):
    k = x0.shape[0]
    step = chunk(k)
    low, high = pl.ds(0, k), pl.ds(k, k)

    def put(rows, columns, value):
        coarse, fine = halves(value)
        part[0, rows, columns] = coarse
        part[1, rows, columns] = fine

    cut(hp, x0[...])
    cut(ap, g[:k, k:])

    def h_rows(rows):
        cut(xp, joined(hp, ap, rows), rows)

    by_rows(k, step, h_rows)
    for index in range(3):
        hp[index] = xp[index]
    cut(xp, x1[...])

    def right_rows(rows):
        put(rows, high, -joined(hp, xp, rows))
        put(below(rows, k), high, x1[rows, :])

    by_rows(k, step, right_rows)

    def a_rows(rows):
        value = joined(xp, ap, rows)
        put(below(rows, k), low, -value)
        cut(tp, value, rows)

    cut(ap, carry[...])
    by_rows(k, step, a_rows)

    def left_rows(rows):
        put(rows, low, x0[rows, :] + joined(hp, tp, rows))

    by_rows(k, step, left_rows)

    def slot_rows(rows):
        picks = back[rows, :]
        coarse, fine = halves(plain(picks, part[0]) + plain(picks, part[1]))
        moved = plain(coarse, spots[...]) + plain(fine, spots[...])
        coarse_out[rows, :], fine_out[rows, :] = halves(moved)

    by_rows(back.shape[0], chunk(back.shape[0]), slot_rows)


def gain(slotted, place, spots, back, variance):
    slots, both = slotted.shape
    k = both // 2
    square = ((k, k), jnp.float32)
    terms = ((3, k, k), jnp.bfloat16)
    (g,) = whole_call(
        assemble_kernel,
        [((both, both), jnp.float32)],
        [((3, slots, both), jnp.bfloat16)],
        slotted,
        place,
        cost=17,
    )

    def inverse(block, b):
        scratch = [square, terms, terms, terms]
        return whole_call(
            invert_kernel, [square], scratch, block, variance[b : b + 1], cost=21
        )[0]

    x0 = inverse(g[:k, :k], 0)
    carry, block = whole_call(deflate_kernel, [square, square], [terms, terms], g, x0, cost=7)
    x1 = inverse(block, 1)
    out = ((slots, spots.shape[1]), jnp.bfloat16)
    return whole_call(
        gain_kernel,
        [out, out],
        [terms] * 4 + [((2, both, both), jnp.bfloat16)],
        g,
        x0,
        x1,
        carry,
        spots,
        back,
        cost=26,
    )


def crossing_kernel(known, slotted, send, recv, side_send, side_recv):
    size = lax.axis_size("col")
    half, side = known.shape[0] // 2, known.shape[1] // 2
    row, col = lax.axis_index("row"), lax.axis_index("col")
    core = row % 2
    even = col % 2 == 0
    ahead = jnp.where(
        even,
        jnp.where(col + 2 < size, col + 2, col + 1),
        jnp.where(col > 1, col - 2, col - 1),
    )
    behind = jnp.where(
        even,
        jnp.where(col > 1, col - 2, col + 1),
        jnp.where(col + 2 < size, col + 2, col - 1),
    )
    partner = row + 1 - 2 * core
    mesh_ids = pl.DeviceIdType.MESH
    barrier = pltpu.get_barrier_semaphore()
    for device in ({"col": ahead}, {"col": behind}, {"row": partner}):
        pl.semaphore_signal(barrier, inc=1, device_id=device, device_id_type=mesh_ids)
    pl.semaphore_wait(barrier, 3)
    columns = pl.ds(pl.multiple_of(core * side, side), side)

    def slot(way, step):
        return slotted.at[pl.ds((2 * step + way) * half, half), columns]

    def source(way, step):
        if step == 0:
            return known.at[pl.ds(way * half, half), columns]
        return slot(way, step)

    copies, sides = {}, []
    for step in range(size):
        for way, device in ((0, {"col": ahead}), (1, {"col": behind})):
            if step:
                copies[way, step - 1].wait_recv()
            if step < size - 1:
                copy = pltpu.make_async_remote_copy(
                    src_ref=source(way, step),
                    dst_ref=slot(way, step + 1),
                    send_sem=send.at[way, step],
                    recv_sem=recv.at[way, step],
                    device_id=device,
                    device_id_type=mesh_ids,
                )
                copy.start()
                copies[way, step] = copy
            copy = pltpu.make_async_remote_copy(
                src_ref=source(way, step),
                dst_ref=slot(way, step),
                send_sem=side_send.at[way, step],
                recv_sem=side_recv.at[way, step],
                device_id={"row": partner},
                device_id_type=mesh_ids,
            )
            copy.start()
            sides.append(copy)
            if step == 0:
                slotted[pl.ds(way * half, half), columns] = known[
                    pl.ds(way * half, half), columns
                ]
    for copy in copies.values():
        copy.wait_send()
    for copy in sides:
        copy.wait()


def crossing_gather(known):
    size = lax.axis_size("col")
    whole = pl.BlockSpec(memory_space=pltpu.VMEM)
    sems = pltpu.SemaphoreType.DMA((2, size))
    return pl.pallas_call(
        crossing_kernel,
        in_specs=[whole],
        out_specs=whole,
        out_shape=jax.ShapeDtypeStruct((known.shape[0] * size, known.shape[1]), known.dtype),
        scratch_shapes=[sems] * 4,
        compiler_params=pltpu.CompilerParams(collective_id=0, has_side_effects=True),
    )(known)


def weights_kernel(gain_coarse, gain_fine, *refs):
    panels, (coarse_out, fine_out) = refs[:-2], refs[-2:]
    coarse, fine = halves(jnp.concatenate([panel[...] for panel in panels], axis=0))

    def write(rows):
        value = plain(gain_coarse[rows, :], coarse)
        value += plain(gain_coarse[rows, :], fine) + plain(gain_fine[rows, :], coarse)
        coarse_out[rows, :], fine_out[rows, :] = halves(value)

    by_rows(gain_coarse.shape[0], gain_coarse.shape[0], write)


def weights_of(gain_coarse, gain_fine, panels):
    slots = gain_coarse.shape[0]
    cols = panels[0].shape[1]
    wide = min(256, cols)
    held = pl.BlockSpec(gain_coarse.shape, lambda j: (0, 0), pipeline_mode=pl.Buffered(1))
    out = jax.ShapeDtypeStruct((slots, cols), jnp.bfloat16)
    return pl.pallas_call(
        weights_kernel,
        grid=(cols // wide,),
        in_specs=[held, held]
        + [pl.BlockSpec((p.shape[0], wide), lambda j: (0, j)) for p in panels],
        out_specs=[pl.BlockSpec((slots, wide), lambda j: (0, j))] * 2,
        out_shape=[out, out],
        cost_estimate=pl.CostEstimate(
            flops=6 * slots * gain_coarse.shape[1] * cols,
            bytes_accessed=12 * slots * cols,
            transcendentals=0,
        ),
        compiler_params=pltpu.CompilerParams(vmem_limit_bytes=60 << 20),
    )(gain_coarse, gain_fine, *panels)


def update_kernel(field, weights_coarse, weights_fine, *refs):
    panels, out = refs[:-1], refs[-1]
    panel = jnp.concatenate([part[...] for part in panels], axis=0).T
    coarse, fine = halves(panel)
    wide = min(512, out.shape[1])

    for index in range(out.shape[1] // wide):
        columns = pl.ds(index * wide, wide)
        value = plain(coarse, weights_coarse[:, columns])
        value += plain(coarse, weights_fine[:, columns])
        value += plain(fine, weights_coarse[:, columns])
        out[:, columns] = field[:, columns] - value


def update(field, weights_coarse, weights_fine, panels, piece):
    rows, cols = field.shape
    tall = min(256, rows)
    tile = pl.BlockSpec((tall, cols), lambda i: (i, 0))
    slots = len(panels) * panels[0].shape[0]
    held = pl.BlockSpec((slots, cols), lambda i: (piece, 0), pipeline_mode=pl.Buffered(1))
    return pl.pallas_call(
        update_kernel,
        grid=(rows // tall,),
        in_specs=[tile, held, held]
        + [pl.BlockSpec((p.shape[0], tall), lambda i: (0, i)) for p in panels],
        out_specs=tile,
        out_shape=jax.ShapeDtypeStruct(field.shape, jnp.float32),
        cost_estimate=pl.CostEstimate(
            flops=8 * slots * rows * cols, bytes_accessed=8 * rows * cols, transcendentals=0
        ),
        compiler_params=pltpu.CompilerParams(vmem_limit_bytes=60 << 20),
    )(field, weights_coarse, weights_fine, *panels)


def capacity(total, parts):
    mean = total / parts
    need = math.ceil((mean + 3.0 * math.sqrt(mean * (1 - 1 / parts))) / 16) * 16
    return min(need, total)


def ring_of(size):
    return list(range(0, size, 2)) + list(range(size - 1 - size % 2, 0, -2))


def ring_gather(up_part, down_part, axis, after):
    cycle = ring_of(lax.axis_size(axis))
    ahead = [(cycle[i], cycle[(i + 1) % len(cycle)]) for i in range(len(cycle))]
    behind = [(b, a) for a, b in ahead]
    ups, downs = [up_part], [down_part]
    for _ in range(1, len(cycle)):
        ups.append(lax.ppermute(ups[-1], axis, ahead))
        downs.append(lax.ppermute(downs[-1], axis, behind))
        if len(ups) == 2:
            ups[1], downs[1], after = lax.optimization_barrier((ups[1], downs[1], after))
    return [part for pair in zip(ups, downs) for part in pair], after


def doubling_masks(size):
    masks, reach = [0], size // 2
    while reach:
        masks += [mask ^ reach for mask in masks]
        reach //= 2
    return masks


def doubling_gather(value, axis):
    size = lax.axis_size(axis)
    parts, reach = [value], size // 2
    while reach:
        pairs = [(i, i ^ reach) for i in range(size)]
        parts += [lax.ppermute(part, axis, pairs) for part in parts]
        reach //= 2
    return parts


def lookup(table, index):
    return jnp.sum(
        jnp.where(index[:, None] == jnp.arange(len(table))[None, :], jnp.array(table)[None, :], 0),
        axis=1,
    )


def places(sites, extent):
    owner = sites // extent
    before = jnp.tril(jnp.ones((sites.size, sites.size), jnp.bool_), -1)
    again = (sites[:, None] == sites[None, :]) & before
    fresh = jnp.logical_not(jnp.any(again, axis=1))
    counts = (owner[:, None] == owner[None, :]) & before & fresh[None, :]
    rank = jnp.sum(counts.astype(jnp.int32), axis=1)
    same = sites[:, None] == sites[None, :]
    shared = jnp.sum(jnp.where(same & fresh[None, :], rank[None, :], 0), axis=1)
    return owner, shared, fresh


def local_cells(sites, place, me, extent, count, empty):
    owner, rank, fresh = place
    hit = (fresh & (owner == me))[None, :] & (rank[None, :] == jnp.arange(count)[:, None])
    cell = jnp.sum(jnp.where(hit, (sites - me * extent - empty)[None, :], 0), axis=1)
    return cell + empty


def one_hot(index, count):
    return (index[:, None] == jnp.arange(count)[None, :]).astype(jnp.bfloat16)


def pick_rows(matrix, sites, first_cell):
    count = matrix.shape[0]
    offsets = sites - first_cell
    owned = (offsets >= 0) & (offsets < count)
    picked = matrix[jnp.clip(offsets, 0, count - 1)]
    return jnp.where(owned[:, None], picked, 0.0)


def pick_kernel(cells, chooser, field, picked, crossing, groups, sem):
    count = picked.shape[0]

    def fetch(index, carry):
        group = pl.multiple_of(cells[index] // MARGIN * MARGIN, MARGIN)
        spot = pl.multiple_of(index * MARGIN, MARGIN)
        pltpu.make_async_copy(
            field.at[pl.ds(group, MARGIN)], groups.at[pl.ds(spot, MARGIN)], sem
        ).start()
        return carry

    lax.fori_loop(0, count, fetch, 0)
    pltpu.make_async_copy(groups, groups, sem).wait()

    def settle(index, carry):
        spot = index * MARGIN + lax.rem(cells[index], MARGIN)
        picked[pl.ds(index, 1), :] = groups[pl.ds(spot, 1), :]
        return carry

    lax.fori_loop(0, count, settle, 0, unroll=8)
    value = picked[...]
    total = jnp.zeros(crossing.shape, jnp.float32)
    for _ in range(3):
        term = value.astype(jnp.bfloat16)
        total += across(chooser[...], term)
        value = value - term.astype(jnp.float32)
    crossing[...] = total


def pick(field, cells, chooser):
    count, cols = cells.size, field.shape[1]
    held = pl.BlockSpec(memory_space=pltpu.VMEM)
    return pl.pallas_call(
        pick_kernel,
        in_specs=[
            pl.BlockSpec(memory_space=pltpu.SMEM),
            held,
            pl.BlockSpec(memory_space=pl.ANY),
        ],
        out_specs=[held, held],
        out_shape=[
            jax.ShapeDtypeStruct((count, cols), jnp.float32),
            jax.ShapeDtypeStruct((chooser.shape[0], count), jnp.float32),
        ],
        scratch_shapes=[
            pltpu.VMEM((count * MARGIN, cols), jnp.float32),
            pltpu.SemaphoreType.DMA,
        ],
        cost_estimate=pl.CostEstimate(
            flops=40 * 10**9, bytes_accessed=1 << 20, transcendentals=0
        ),
        compiler_params=pltpu.CompilerParams(vmem_limit_bytes=60 << 20),
    )(cells, chooser, field)


def balanced(prior, prepared, row_sites, col_sites, error_var, row_place, col_place):
    rows, cols = prior.shape
    across_rows, across_cols = lax.axis_size("row"), lax.axis_size("col")
    my_row, my_col = lax.axis_index("row"), lax.axis_index("col")
    total = row_sites.size
    row_slots, col_slots = capacity(total, across_rows), capacity(total, across_cols)
    row_owner, row_rank, _ = row_place
    col_owner, col_rank, _ = col_place
    half = col_slots // 2

    my_rows = local_cells(row_sites, row_place, my_row, rows, row_slots, 0)
    my_cols = local_cells(col_sites, col_place, my_col, cols, col_slots, -1)
    chooser = one_hot(my_cols, cols)

    masks = doubling_masks(across_rows)
    order = [masks.index(mask) for mask in range(across_rows)]
    row_slot = lookup(order, row_owner ^ my_row) * row_slots + row_rank
    cycle = ring_of(across_cols)
    spot = [cycle.index(c) for c in range(across_cols)]
    here = lookup(spot, my_col[None])[0]
    away = lookup(spot, col_owner) - here
    up_step, down_step = (-away) % across_cols, away % across_cols
    col_slot = jnp.where(
        col_rank < half,
        2 * up_step * half + col_rank,
        2 * down_step * half + col_rank,
    )
    spots = one_hot(row_slot, across_rows * row_slots)
    place = one_hot(col_slot, across_cols * col_slots)

    field, up_part, down_part = transport(prior, prepared, chooser, 2)
    row_part, crossing = pick(field, my_rows, chooser)
    pieces = doubling_gather(crossing, "row")
    known = exact(jnp.concatenate(pieces, axis=1), spots.astype(jnp.float32).T)
    row_part, known = lax.optimization_barrier((row_part, known))
    slotted = crossing_gather(known)
    panels = doubling_gather(row_part, "row")
    parts, slotted = ring_gather(up_part, down_part, "col", slotted)
    gain_coarse, gain_fine = gain(slotted, place, spots, place.T, error_var)
    weights = weights_of(gain_coarse, gain_fine, panels)
    last = len(parts) // LAST
    field = update(field, *weights, parts[:-last], 0)
    return update(field, *weights, parts[-last:], LAST - 1)


def added_up(value, axis):
    size, reach = lax.axis_size(axis), 1
    while reach < size:
        pairs = [(i, i ^ reach) for i in range(size)]
        value = value + lax.ppermute(value, axis, pairs)
        reach *= 2
    return value


def product_kernel(left, right, out):
    out[...] = exact(left[...], right[...])


def product(left, right):
    (rows, depth), cols = left.shape, right.shape[1]
    tall, wide = min(256, rows), min(256, cols)
    return pl.pallas_call(
        product_kernel,
        grid=(rows // tall, cols // wide),
        in_specs=[
            pl.BlockSpec((tall, depth), lambda i, j: (i, 0)),
            pl.BlockSpec((depth, wide), lambda i, j: (0, j)),
        ],
        out_specs=pl.BlockSpec((tall, wide), lambda i, j: (i, j)),
        out_shape=jax.ShapeDtypeStruct((rows, cols), jnp.float32),
    )(left, right)


def newton(matrix):
    unit = jnp.eye(matrix.shape[0], dtype=jnp.float32)

    def more(state):
        index, _, norm = state
        return (index < 60) & jnp.logical_not(norm < 1e-7)

    def step(state):
        index, inverse, _ = state
        error = unit - product(matrix, inverse)
        return index + 1, inverse + product(inverse, error), jnp.sum(error * error)

    inverse = unit / jnp.max(jnp.sum(jnp.abs(matrix), axis=0))
    return lax.while_loop(more, step, (jnp.int32(0), inverse, jnp.float32(1.0)))[1]


def crowded(prior, prepared, row_sites, col_sites, error_var, row_place, col_place):
    rows, cols = prior.shape
    row_first = lax.axis_index("row") * rows
    col_first = lax.axis_index("col") * cols
    k = error_var.shape[1]
    chooser = one_hot(col_sites - col_first, cols)
    field, picked = transport(prior, prepared, chooser, 1)
    row_part = pick_rows(field, row_sites, row_first)
    crossing = product(row_part, chooser.astype(jnp.float32).T)
    crossing = added_up(added_up(crossing, "row"), "col")
    row_panel = added_up(row_part, "row")
    column_panel = added_up(picked, "col")

    def body(b, state):
        crossing, row_panel, column_panel, field = state
        mine = b * k
        block = lax.dynamic_slice(crossing, (mine, mine), (k, k))
        variance = lax.dynamic_index_in_dim(error_var, b, 0, keepdims=False)
        inverse = newton(jnp.diag(variance) + product(block, block.T))
        picked_rows = lax.dynamic_slice_in_dim(row_panel, mine, k, axis=0)
        picked_cols = lax.dynamic_slice_in_dim(column_panel, mine, k, axis=0).T
        weights = product(inverse, picked_rows)
        field = field - product(picked_cols, weights)
        cross_rows = lax.dynamic_slice_in_dim(crossing, mine, k, axis=0)
        cross_cols = lax.dynamic_slice_in_dim(crossing, mine, k, axis=1)
        row_panel = row_panel - product(cross_cols, weights)
        gains = product(inverse, cross_rows)
        column_panel = column_panel - product(gains.T, picked_cols.T)
        return crossing - product(cross_cols, gains), row_panel, column_panel, field

    state = (crossing, row_panel, column_panel, field)
    return lax.fori_loop(0, error_var.shape[0], body, state)[3]


def shards(
    prior,
    ozone_courant,
    ozone_diffusion,
    ozone_wind,
    carbon_courant,
    carbon_diffusion,
    carbon_wind,
    ozone_sites,
    carbon_sites,
    error_var,
):
    rows, cols = prior.shape
    row_sites = ozone_sites.reshape(-1)
    col_sites = carbon_sites.reshape(-1)
    ozone = (ozone_courant, ozone_diffusion, ozone_wind)
    carbon = (carbon_courant, carbon_diffusion, carbon_wind)
    row_place = places(row_sites, rows)
    col_place = places(col_sites, cols)
    total = row_sites.size
    fits = (jnp.max(row_place[1]) < capacity(total, lax.axis_size("row"))) & (
        jnp.max(col_place[1]) < capacity(total, lax.axis_size("col"))
    )
    prepared = surroundings(
        prior, ozone, carbon, lax.axis_index("row") * rows, lax.axis_index("col") * cols
    )
    given = (prior, prepared, row_sites, col_sites, error_var, row_place, col_place)
    return lax.cond(fits, balanced, crowded, *given)


def solution(mesh):
    placed = (P("row", "col"), P(), P(), P(), P(), P(), P(), P(), P(), P())
    return jax.shard_map(
        shards, mesh=mesh, in_specs=placed, out_specs=P("row", "col"), check_vma=False
    )
```

```python
import math
import jax
import jax.numpy as jnp
from jax import lax
from jax.experimental import pallas as pl
from jax.experimental.pallas import tpu as pltpu
from jax.sharding import PartitionSpec as P

STEPS = 2
MARGIN = 8
LANES = 128
TILE = 256
HIGHEST = lax.Precision.HIGHEST
LAST = 4
SCALE = 1.5


def coefficients(courant, diffusion, wind, first_cell, before, after, count):
    pad = (before, after)
    total = count + before + after

    def cut(values):
        return lax.dynamic_slice_in_dim(jnp.pad(values, pad), first_cell, total)

    c, d, w = cut(courant), cut(diffusion), cut(wind)
    low = d + jnp.where(w == 0, c, 0.0)
    high = d + jnp.where(w == 0, 0.0, c)
    return low, 1.0 - c - 2.0 * d, high


def edges(value, axis, dim, width):
    size, length = lax.axis_size(axis), value.shape[dim]
    up = [(i, i + 1) for i in range(size - 1)]
    down = [(i + 1, i) for i in range(size - 1)]
    last = lax.slice_in_dim(value, length - width, length, axis=dim)
    leading = lax.slice_in_dim(value, 0, width, axis=dim)
    return lax.ppermute(last, axis, up), lax.ppermute(leading, axis, down)


def across(left, right):
    return lax.dot_general(
        left, right, (((1,), (1,)), ((), ())), preferred_element_type=jnp.float32
    )


def transport_kernel(main, prev, follow, above, below, side, row_weights, col_weights, chooser, out, *picked):
    step = pl.program_id(0)
    last = pl.num_programs(0) - 1
    top = jnp.where(step == 0, above[...], prev[...])
    bottom = jnp.where(step == last, below[...], follow[...])
    body = jnp.concatenate([top, main[...], bottom], axis=0)
    value = jnp.concatenate([body, side[0]], axis=1)
    weights = row_weights[0]
    low, mid, high = weights[:, 0:1], weights[:, 1:2], weights[:, 2:3]
    rows = value.shape[0]
    for _ in range(STEPS):
        value = low * pltpu.roll(value, 1, 0) + mid * value + high * pltpu.roll(value, rows - 1, 0)
    value = value[MARGIN : rows - MARGIN]
    width = value.shape[1]
    low, mid, high = col_weights[0:1], col_weights[1:2], col_weights[2:3]
    for _ in range(STEPS):
        value = low * pltpu.roll(value, 1, 1) + mid * value + high * pltpu.roll(value, width - 1, 1)
    value = value[:, : out.shape[1]]
    out[...] = value
    coarse = value.astype(jnp.bfloat16)
    fine = (value - coarse.astype(jnp.float32)).astype(jnp.bfloat16)
    chosen = across(chooser[...], coarse) + across(chooser[...], fine)
    count = chosen.shape[0] // len(picked)
    for index, part in enumerate(picked):
        part[...] = chosen[index * count : (index + 1) * count]


def surroundings(prior, ozone, carbon, row_first, col_first):
    rows, cols = prior.shape
    tiles, per = rows // TILE, TILE // MARGIN
    above, below = edges(prior, "row", 0, MARGIN)
    left, right = edges(prior, "col", 1, STEPS)
    strips = jnp.concatenate([right, left], axis=1)
    strip_above, strip_below = edges(strips, "row", 0, MARGIN)
    strips = jnp.concatenate([strip_above, strips, strip_below], axis=0)
    strips = jnp.concatenate(
        [
            strips[:, :STEPS],
            jnp.zeros((strips.shape[0], LANES - 2 * STEPS), jnp.float32),
            strips[:, STEPS:],
        ],
        axis=1,
    )

    def windows(values):
        parts = values.reshape((tiles * per + 2, MARGIN) + values.shape[1:])
        main = parts[: tiles * per].reshape((tiles, TILE) + values.shape[1:])
        tail = parts[per:].reshape((-1,) + values.shape[1:])
        tail = jnp.stack([tail[i * TILE : i * TILE + 2 * MARGIN] for i in range(tiles)])
        return jnp.concatenate([main, tail], axis=1)

    side = windows(strips)
    row_weights = windows(
        jnp.stack(coefficients(*ozone, row_first, MARGIN, MARGIN, rows), axis=1)
    )
    row_weights = jnp.pad(row_weights, ((0, 0), (0, 0), (0, 5)))
    trio = coefficients(*carbon, col_first, STEPS, STEPS, cols)
    rolled = []
    for entry in trio:
        filler = jnp.zeros((LANES - 2 * STEPS,), jnp.float32)
        rolled.append(jnp.concatenate([entry[STEPS:], filler, entry[:STEPS]]))
    col_weights = jnp.pad(jnp.stack(rolled), ((0, 5), (0, 0)))
    return above, below, side, row_weights, col_weights


def transport(prior, prepared, chooser, pieces):
    rows, cols = prior.shape
    tiles, per = rows // TILE, TILE // MARGIN
    extent = TILE + 2 * MARGIN
    count = chooser.shape[0] // pieces
    blocks = rows // MARGIN
    return pl.pallas_call(
        transport_kernel,
        grid=(tiles,),
        in_specs=[
            pl.BlockSpec((TILE, cols), lambda i: (i, 0)),
            pl.BlockSpec((MARGIN, cols), lambda i: (jnp.maximum(i * per - 1, 0), 0)),
            pl.BlockSpec((MARGIN, cols), lambda i: (jnp.minimum((i + 1) * per, blocks - 1), 0)),
            pl.BlockSpec((MARGIN, cols), lambda i: (0, 0)),
            pl.BlockSpec((MARGIN, cols), lambda i: (0, 0)),
            pl.BlockSpec((1, extent, LANES), lambda i: (i, 0, 0)),
            pl.BlockSpec((1, extent, 8), lambda i: (i, 0, 0)),
            pl.BlockSpec((8, cols + LANES), lambda i: (0, 0)),
            pl.BlockSpec(chooser.shape, lambda i: (0, 0)),
        ],
        out_specs=[
            pl.BlockSpec((TILE, cols), lambda i: (i, 0)),
        ]
        + [pl.BlockSpec((count, TILE), lambda i: (0, i))] * pieces,
        out_shape=[
            jax.ShapeDtypeStruct((rows, cols), jnp.float32),
        ]
        + [jax.ShapeDtypeStruct((count, rows), jnp.float32)] * pieces,
        compiler_params=pltpu.CompilerParams(vmem_limit_bytes=60 << 20),
    )(prior, prior, prior, *prepared, chooser)


def plain(first_matrix, second_matrix):
    return jnp.dot(first_matrix, second_matrix, preferred_element_type=jnp.float32)


def exact(first_matrix, second_matrix):
    return jnp.dot(
        first_matrix, second_matrix, precision=HIGHEST, preferred_element_type=jnp.float32
    )


def halves(value):
    coarse = value.astype(jnp.bfloat16)
    return coarse, (value - coarse.astype(jnp.float32)).astype(jnp.bfloat16)


def by_rows(count, step, write):
    def body(index, carry):
        write(pl.ds(pl.multiple_of(index * step, step), step))
        return carry

    lax.fori_loop(0, count // step, body, 0)


def chunk(count):
    return next(n for n in (512, 640, 256, 128, 16) if count % n == 0)


def below(rows, first):
    return pl.ds(rows.start + first, rows.size)


def unit_rows(rows, k):
    down = lax.broadcasted_iota(jnp.int32, (rows.size, k), 0) + rows.start
    return (down == lax.broadcasted_iota(jnp.int32, (rows.size, k), 1)).astype(jnp.float32)


def cut(parts, value, rows=slice(None)):
    for index in range(parts.shape[0]):
        term = value.astype(jnp.bfloat16)
        parts[index, rows, :] = term
        value = value - term.astype(jnp.float32)


def joined(left, right, rows, product=plain):
    small = product(left[0, rows, :], right[2]) + product(left[2, rows, :], right[0])
    small += product(left[1, rows, :], right[1])
    small += product(left[0, rows, :], right[1]) + product(left[1, rows, :], right[0])
    return small + product(left[0, rows, :], right[0])


def whole_call(kernel, outs, scratch, *args, cost):
    whole = pl.BlockSpec(memory_space=pltpu.VMEM)
    return pl.pallas_call(
        kernel,
        in_specs=[whole] * len(args),
        out_specs=[whole] * len(outs),
        out_shape=[jax.ShapeDtypeStruct(*out) for out in outs],
        scratch_shapes=[pltpu.VMEM(*entry) for entry in scratch],
        cost_estimate=pl.CostEstimate(
            flops=int(cost * SCALE * 1e9), bytes_accessed=1 << 20, transcendentals=0
        ),
        compiler_params=pltpu.CompilerParams(vmem_limit_bytes=60 << 20),
    )(*args)


def assemble_kernel(slotted, place, g, parts):
    cut(parts, slotted[...])

    def write(rows):
        picks = place[rows, :]
        g[rows, :] = plain(picks, parts[0]) + plain(picks, parts[1]) + plain(picks, parts[2])

    by_rows(g.shape[0], chunk(g.shape[0]), write)
    g[...] = g[...].T


def invert_kernel(block, variance, x, s, sp, xp, ep):
    k = s.shape[0]
    step = chunk(k)
    cut(xp, block[:k, :k])

    def innovation(rows):
        s[rows, :] = unit_rows(rows, k) * variance[...] + joined(xp, xp, rows, across)

    by_rows(k, step, innovation)
    cut(sp, s[...])
    bound = jnp.max(jnp.sum(jnp.abs(s[...]), axis=0))

    def begin():
        x[...] = (1.0 / bound) * unit_rows(pl.ds(0, k), k)
        cut(xp, x[...])

    def residual(precise):
        def body(index, total):
            rows = pl.ds(pl.multiple_of(index * step, step), step)
            if precise:
                left = unit_rows(rows, k) - joined(sp, xp, rows)
                cut(ep, left, rows)
            else:
                left = unit_rows(rows, k) - plain(sp[0, rows, :], xp[0])
                ep[0, rows, :] = left.astype(jnp.bfloat16)
            return total + jnp.sum(left * left)

        return lax.fori_loop(0, k // step, body, jnp.float32(0.0))

    def improve(precise):
        def write(rows):
            value = plain(xp[0, rows, :], ep[0])
            if precise:
                value += plain(xp[0, rows, :], ep[1]) + plain(xp[1, rows, :], ep[0])
            value += x[rows, :]
            x[rows, :] = value
            if precise:
                cut(xp, value, rows)
            else:
                xp[0, rows, :] = value.astype(jnp.bfloat16)

        by_rows(k, step, write)

    begin()
    first = residual(False)

    def coarse_more(state):
        index, norm = state
        return (index < 14) & (norm > 0.25) & (norm <= 1.1 * first)

    def coarse_step(state):
        index, _ = state
        improve(False)
        return index + 1, residual(False)

    lax.while_loop(coarse_more, coarse_step, (jnp.int32(0), first))
    cut(xp, x[...])

    def fine_more(state):
        index, norm = state
        return (index < 60) & jnp.logical_not(norm < 1e-5)

    def fine_step(state):
        index, norm = state

        @pl.when((index == 0) | (norm < 0.8) | (index > 1))
        def _():
            @pl.when(index > 0)
            def _():
                improve(True)

        @pl.when((index == 1) & jnp.logical_not(norm < 0.8))
        def _():
            begin()

        return index + 1, residual(True)

    lax.while_loop(fine_more, fine_step, (jnp.int32(0), jnp.float32(1.0)))
    improve(True)


def deflate_kernel(g, x0, carry, block, left, right):
    k = x0.shape[0]
    step = chunk(k)
    cut(left, g[k:, :k])
    cut(right, x0[...])

    def carry_rows(rows):
        carry[rows, :] = joined(left, right, rows)

    by_rows(k, step, carry_rows)
    cut(left, carry[...])
    cut(right, g[:k, k:])

    def block_rows(rows):
        block[rows, :] = g[below(rows, k), k:] - joined(left, right, rows)

    by_rows(k, step, block_rows)


def gain_kernel(g, x0, x1, carry, spots, back, coarse_out, fine_out, hp, ap, xp, tp, part):
    k = x0.shape[0]
    step = chunk(k)
    low, high = pl.ds(0, k), pl.ds(k, k)

    def put(rows, columns, value):
        coarse, fine = halves(value)
        part[0, rows, columns] = coarse
        part[1, rows, columns] = fine

    cut(hp, x0[...])
    cut(ap, g[:k, k:])

    def h_rows(rows):
        cut(xp, joined(hp, ap, rows), rows)

    by_rows(k, step, h_rows)
    for index in range(3):
        hp[index] = xp[index]
    cut(xp, x1[...])

    def right_rows(rows):
        put(rows, high, -joined(hp, xp, rows))
        put(below(rows, k), high, x1[rows, :])

    by_rows(k, step, right_rows)

    def a_rows(rows):
        value = joined(xp, ap, rows)
        put(below(rows, k), low, -value)
        cut(tp, value, rows)

    cut(ap, carry[...])
    by_rows(k, step, a_rows)

    def left_rows(rows):
        put(rows, low, x0[rows, :] + joined(hp, tp, rows))

    by_rows(k, step, left_rows)

    def slot_rows(rows):
        picks = back[rows, :]
        coarse, fine = halves(plain(picks, part[0]) + plain(picks, part[1]))
        moved = plain(coarse, spots[...]) + plain(fine, spots[...])
        coarse_out[rows, :], fine_out[rows, :] = halves(moved)

    by_rows(back.shape[0], chunk(back.shape[0]), slot_rows)


def gain(slotted, place, spots, back, variance):
    slots, both = slotted.shape
    k = both // 2
    square = ((k, k), jnp.float32)
    terms = ((3, k, k), jnp.bfloat16)
    (g,) = whole_call(
        assemble_kernel,
        [((both, both), jnp.float32)],
        [((3, slots, both), jnp.bfloat16)],
        slotted,
        place,
        cost=17,
    )

    def inverse(block, b):
        scratch = [square, terms, terms, terms]
        return whole_call(
            invert_kernel, [square], scratch, block, variance[b : b + 1], cost=21
        )[0]

    x0 = inverse(g, 0)
    carry, block = whole_call(deflate_kernel, [square, square], [terms, terms], g, x0, cost=7)
    x1 = inverse(block, 1)
    out = ((slots, spots.shape[1]), jnp.bfloat16)
    return whole_call(
        gain_kernel,
        [out, out],
        [terms] * 4 + [((2, both, both), jnp.bfloat16)],
        g,
        x0,
        x1,
        carry,
        spots,
        back,
        cost=26,
    )


def crossing_kernel(known, slotted, send, recv, side_send, side_recv):
    size = lax.axis_size("col")
    half, side = known.shape[0] // 2, known.shape[1] // 2
    row, col = lax.axis_index("row"), lax.axis_index("col")
    core = row % 2
    even = col % 2 == 0
    ahead = jnp.where(
        even,
        jnp.where(col + 2 < size, col + 2, col + 1),
        jnp.where(col > 1, col - 2, col - 1),
    )
    behind = jnp.where(
        even,
        jnp.where(col > 1, col - 2, col + 1),
        jnp.where(col + 2 < size, col + 2, col - 1),
    )
    partner = row + 1 - 2 * core
    mesh_ids = pl.DeviceIdType.MESH
    barrier = pltpu.get_barrier_semaphore()
    for device in ({"col": ahead}, {"col": behind}, {"row": partner}):
        pl.semaphore_signal(barrier, inc=1, device_id=device, device_id_type=mesh_ids)
    pl.semaphore_wait(barrier, 3)
    columns = pl.ds(pl.multiple_of(core * side, side), side)

    def slot(way, step):
        return slotted.at[pl.ds((2 * step + way) * half, half), columns]

    def source(way, step):
        if step == 0:
            return known.at[pl.ds(way * half, half), columns]
        return slot(way, step)

    copies, sides = {}, []
    for step in range(size):
        for way, device in ((0, {"col": ahead}), (1, {"col": behind})):
            if step:
                copies[way, step - 1].wait_recv()
            if step < size - 1:
                copy = pltpu.make_async_remote_copy(
                    src_ref=source(way, step),
                    dst_ref=slot(way, step + 1),
                    send_sem=send.at[way, step],
                    recv_sem=recv.at[way, step],
                    device_id=device,
                    device_id_type=mesh_ids,
                )
                copy.start()
                copies[way, step] = copy
            copy = pltpu.make_async_remote_copy(
                src_ref=source(way, step),
                dst_ref=slot(way, step),
                send_sem=side_send.at[way, step],
                recv_sem=side_recv.at[way, step],
                device_id={"row": partner},
                device_id_type=mesh_ids,
            )
            copy.start()
            sides.append(copy)
            if step == 0:
                slotted[pl.ds(way * half, half), columns] = known[
                    pl.ds(way * half, half), columns
                ]
    for copy in copies.values():
        copy.wait_send()
    for copy in sides:
        copy.wait()


def crossing_gather(known):
    size = lax.axis_size("col")
    whole = pl.BlockSpec(memory_space=pltpu.VMEM)
    sems = pltpu.SemaphoreType.DMA((2, size))
    return pl.pallas_call(
        crossing_kernel,
        in_specs=[whole],
        out_specs=whole,
        out_shape=jax.ShapeDtypeStruct((known.shape[0] * size, known.shape[1]), known.dtype),
        scratch_shapes=[sems] * 4,
        compiler_params=pltpu.CompilerParams(collective_id=0, has_side_effects=True),
    )(known)


def weights_kernel(gain_coarse, gain_fine, *refs):
    panels, (coarse_out, fine_out) = refs[:-2], refs[-2:]
    coarse, fine = halves(jnp.concatenate([panel[...] for panel in panels], axis=0))

    def write(rows):
        value = plain(gain_coarse[rows, :], coarse)
        value += plain(gain_coarse[rows, :], fine) + plain(gain_fine[rows, :], coarse)
        coarse_out[rows, :], fine_out[rows, :] = halves(value)

    by_rows(gain_coarse.shape[0], gain_coarse.shape[0], write)


def weights_of(gain_coarse, gain_fine, panels):
    slots = gain_coarse.shape[0]
    cols = panels[0].shape[1]
    wide = min(256, cols)
    held = pl.BlockSpec(gain_coarse.shape, lambda j: (0, 0), pipeline_mode=pl.Buffered(1))
    out = jax.ShapeDtypeStruct((slots, cols), jnp.bfloat16)
    return pl.pallas_call(
        weights_kernel,
        grid=(cols // wide,),
        in_specs=[held, held]
        + [pl.BlockSpec((p.shape[0], wide), lambda j: (0, j)) for p in panels],
        out_specs=[pl.BlockSpec((slots, wide), lambda j: (0, j))] * 2,
        out_shape=[out, out],
        cost_estimate=pl.CostEstimate(
            flops=6 * slots * gain_coarse.shape[1] * cols,
            bytes_accessed=12 * slots * cols,
            transcendentals=0,
        ),
        compiler_params=pltpu.CompilerParams(vmem_limit_bytes=60 << 20),
    )(gain_coarse, gain_fine, *panels)


def update_kernel(field, weights_coarse, weights_fine, *refs):
    panels, out = refs[:-1], refs[-1]
    panel = jnp.concatenate([part[...] for part in panels], axis=0).T
    coarse, fine = halves(panel)
    wide = min(512, out.shape[1])

    for index in range(out.shape[1] // wide):
        columns = pl.ds(index * wide, wide)
        value = plain(coarse, weights_coarse[:, columns])
        value += plain(coarse, weights_fine[:, columns])
        value += plain(fine, weights_coarse[:, columns])
        out[:, columns] = field[:, columns] - value


def update(field, weights_coarse, weights_fine, panels, piece):
    rows, cols = field.shape
    tall = min(256, rows)
    tile = pl.BlockSpec((tall, cols), lambda i: (i, 0))
    slots = len(panels) * panels[0].shape[0]
    held = pl.BlockSpec((slots, cols), lambda i: (piece, 0), pipeline_mode=pl.Buffered(1))
    return pl.pallas_call(
        update_kernel,
        grid=(rows // tall,),
        in_specs=[tile, held, held]
        + [pl.BlockSpec((p.shape[0], tall), lambda i: (0, i)) for p in panels],
        out_specs=tile,
        out_shape=jax.ShapeDtypeStruct(field.shape, jnp.float32),
        cost_estimate=pl.CostEstimate(
            flops=8 * slots * rows * cols, bytes_accessed=8 * rows * cols, transcendentals=0
        ),
        compiler_params=pltpu.CompilerParams(vmem_limit_bytes=60 << 20),
    )(field, weights_coarse, weights_fine, *panels)


def capacity(total, parts):
    mean = total / parts
    need = math.ceil((mean + 3.0 * math.sqrt(mean * (1 - 1 / parts))) / 16) * 16
    return min(need, total)


def ring_of(size):
    return list(range(0, size, 2)) + list(range(size - 1 - size % 2, 0, -2))


def ring_gather(up_part, down_part, axis, after):
    cycle = ring_of(lax.axis_size(axis))
    ahead = [(cycle[i], cycle[(i + 1) % len(cycle)]) for i in range(len(cycle))]
    behind = [(b, a) for a, b in ahead]
    ups, downs = [up_part], [down_part]
    for _ in range(1, len(cycle)):
        ups.append(lax.ppermute(ups[-1], axis, ahead))
        downs.append(lax.ppermute(downs[-1], axis, behind))
        if len(ups) == 2:
            ups[1], downs[1], after = lax.optimization_barrier((ups[1], downs[1], after))
    return [part for pair in zip(ups, downs) for part in pair], after


def doubling_masks(size):
    masks, reach = [0], size // 2
    while reach:
        masks += [mask ^ reach for mask in masks]
        reach //= 2
    return masks


def doubling_gather(value, axis):
    size = lax.axis_size(axis)
    parts, reach = [value], size // 2
    while reach:
        pairs = [(i, i ^ reach) for i in range(size)]
        parts += [lax.ppermute(part, axis, pairs) for part in parts]
        reach //= 2
    return parts


def lookup(table, index):
    return jnp.sum(
        jnp.where(index[:, None] == jnp.arange(len(table))[None, :], jnp.array(table)[None, :], 0),
        axis=1,
    )


def places(sites, extent):
    owner = sites // extent
    before = jnp.tril(jnp.ones((sites.size, sites.size), jnp.bool_), -1)
    again = (sites[:, None] == sites[None, :]) & before
    fresh = jnp.logical_not(jnp.any(again, axis=1))
    counts = (owner[:, None] == owner[None, :]) & before & fresh[None, :]
    rank = jnp.sum(counts.astype(jnp.int32), axis=1)
    same = sites[:, None] == sites[None, :]
    shared = jnp.sum(jnp.where(same & fresh[None, :], rank[None, :], 0), axis=1)
    return owner, shared, fresh


def local_cells(sites, place, me, extent, count, empty):
    owner, rank, fresh = place
    hit = (fresh & (owner == me))[None, :] & (rank[None, :] == jnp.arange(count)[:, None])
    cell = jnp.sum(jnp.where(hit, (sites - me * extent - empty)[None, :], 0), axis=1)
    return cell + empty


def one_hot(index, count):
    return (index[:, None] == jnp.arange(count)[None, :]).astype(jnp.bfloat16)


def pick_rows(matrix, sites, first_cell):
    count = matrix.shape[0]
    offsets = sites - first_cell
    owned = (offsets >= 0) & (offsets < count)
    picked = matrix[jnp.clip(offsets, 0, count - 1)]
    return jnp.where(owned[:, None], picked, 0.0)


def pick_kernel(cells, chooser, field, picked, crossing, groups, sem):
    count = picked.shape[0]

    def fetch(index, carry):
        group = pl.multiple_of(cells[index] // MARGIN * MARGIN, MARGIN)
        spot = pl.multiple_of(index * MARGIN, MARGIN)
        pltpu.make_async_copy(
            field.at[pl.ds(group, MARGIN)], groups.at[pl.ds(spot, MARGIN)], sem
        ).start()
        return carry

    lax.fori_loop(0, count, fetch, 0)
    pltpu.make_async_copy(groups, groups, sem).wait()

    def settle(index, carry):
        spot = index * MARGIN + lax.rem(cells[index], MARGIN)
        picked[pl.ds(index, 1), :] = groups[pl.ds(spot, 1), :]
        return carry

    lax.fori_loop(0, count, settle, 0, unroll=8)
    value = picked[...]
    total = jnp.zeros(crossing.shape, jnp.float32)
    for _ in range(3):
        term = value.astype(jnp.bfloat16)
        total += across(chooser[...], term)
        value = value - term.astype(jnp.float32)
    crossing[...] = total


def pick(field, cells, chooser):
    count, cols = cells.size, field.shape[1]
    held = pl.BlockSpec(memory_space=pltpu.VMEM)
    return pl.pallas_call(
        pick_kernel,
        in_specs=[
            pl.BlockSpec(memory_space=pltpu.SMEM),
            held,
            pl.BlockSpec(memory_space=pl.ANY),
        ],
        out_specs=[held, held],
        out_shape=[
            jax.ShapeDtypeStruct((count, cols), jnp.float32),
            jax.ShapeDtypeStruct((chooser.shape[0], count), jnp.float32),
        ],
        scratch_shapes=[
            pltpu.VMEM((count * MARGIN, cols), jnp.float32),
            pltpu.SemaphoreType.DMA,
        ],
        cost_estimate=pl.CostEstimate(
            flops=40 * 10**9, bytes_accessed=1 << 20, transcendentals=0
        ),
        compiler_params=pltpu.CompilerParams(vmem_limit_bytes=60 << 20),
    )(cells, chooser, field)


def balanced(prior, prepared, row_sites, col_sites, error_var, row_place, col_place):
    rows, cols = prior.shape
    across_rows, across_cols = lax.axis_size("row"), lax.axis_size("col")
    my_row, my_col = lax.axis_index("row"), lax.axis_index("col")
    total = row_sites.size
    row_slots, col_slots = capacity(total, across_rows), capacity(total, across_cols)
    row_owner, row_rank, _ = row_place
    col_owner, col_rank, _ = col_place
    half = col_slots // 2

    my_rows = local_cells(row_sites, row_place, my_row, rows, row_slots, 0)
    my_cols = local_cells(col_sites, col_place, my_col, cols, col_slots, -1)
    chooser = one_hot(my_cols, cols)

    masks = doubling_masks(across_rows)
    order = [masks.index(mask) for mask in range(across_rows)]
    row_slot = lookup(order, row_owner ^ my_row) * row_slots + row_rank
    cycle = ring_of(across_cols)
    spot = [cycle.index(c) for c in range(across_cols)]
    here = lookup(spot, my_col[None])[0]
    away = lookup(spot, col_owner) - here
    up_step, down_step = (-away) % across_cols, away % across_cols
    col_slot = jnp.where(
        col_rank < half,
        2 * up_step * half + col_rank,
        2 * down_step * half + col_rank,
    )
    spots = one_hot(row_slot, across_rows * row_slots)
    place = one_hot(col_slot, across_cols * col_slots)

    field, up_part, down_part = transport(prior, prepared, chooser, 2)
    row_part, crossing = pick(field, my_rows, chooser)
    pieces = doubling_gather(crossing, "row")
    known = exact(jnp.concatenate(pieces, axis=1), spots.astype(jnp.float32).T)
    row_part, known = lax.optimization_barrier((row_part, known))
    slotted = crossing_gather(known)
    panels = doubling_gather(row_part, "row")
    parts, slotted = ring_gather(up_part, down_part, "col", slotted)
    gain_coarse, gain_fine = gain(slotted, place, spots, place.T, error_var)
    weights = weights_of(gain_coarse, gain_fine, panels)
    last = len(parts) // LAST
    field = update(field, *weights, parts[:-last], 0)
    return update(field, *weights, parts[-last:], LAST - 1)


def added_up(value, axis):
    size, reach = lax.axis_size(axis), 1
    while reach < size:
        pairs = [(i, i ^ reach) for i in range(size)]
        value = value + lax.ppermute(value, axis, pairs)
        reach *= 2
    return value


def product_kernel(left, right, out):
    out[...] = exact(left[...], right[...])


def product(left, right):
    (rows, depth), cols = left.shape, right.shape[1]
    tall, wide = min(256, rows), min(256, cols)
    return pl.pallas_call(
        product_kernel,
        grid=(rows // tall, cols // wide),
        in_specs=[
            pl.BlockSpec((tall, depth), lambda i, j: (i, 0)),
            pl.BlockSpec((depth, wide), lambda i, j: (0, j)),
        ],
        out_specs=pl.BlockSpec((tall, wide), lambda i, j: (i, j)),
        out_shape=jax.ShapeDtypeStruct((rows, cols), jnp.float32),
    )(left, right)


def newton(matrix):
    unit = jnp.eye(matrix.shape[0], dtype=jnp.float32)

    def more(state):
        index, _, norm = state
        return (index < 60) & jnp.logical_not(norm < 1e-7)

    def step(state):
        index, inverse, _ = state
        error = unit - product(matrix, inverse)
        return index + 1, inverse + product(inverse, error), jnp.sum(error * error)

    inverse = unit / jnp.max(jnp.sum(jnp.abs(matrix), axis=0))
    return lax.while_loop(more, step, (jnp.int32(0), inverse, jnp.float32(1.0)))[1]


def crowded(prior, prepared, row_sites, col_sites, error_var, row_place, col_place):
    rows, cols = prior.shape
    row_first = lax.axis_index("row") * rows
    col_first = lax.axis_index("col") * cols
    k = error_var.shape[1]
    chooser = one_hot(col_sites - col_first, cols)
    field, picked = transport(prior, prepared, chooser, 1)
    row_part = pick_rows(field, row_sites, row_first)
    crossing = product(row_part, chooser.astype(jnp.float32).T)
    crossing = added_up(added_up(crossing, "row"), "col")
    row_panel = added_up(row_part, "row")
    column_panel = added_up(picked, "col")

    def body(b, state):
        crossing, row_panel, column_panel, field = state
        mine = b * k
        block = lax.dynamic_slice(crossing, (mine, mine), (k, k))
        variance = lax.dynamic_index_in_dim(error_var, b, 0, keepdims=False)
        inverse = newton(jnp.diag(variance) + product(block, block.T))
        picked_rows = lax.dynamic_slice_in_dim(row_panel, mine, k, axis=0)
        picked_cols = lax.dynamic_slice_in_dim(column_panel, mine, k, axis=0).T
        weights = product(inverse, picked_rows)
        field = field - product(picked_cols, weights)
        cross_rows = lax.dynamic_slice_in_dim(crossing, mine, k, axis=0)
        cross_cols = lax.dynamic_slice_in_dim(crossing, mine, k, axis=1)
        row_panel = row_panel - product(cross_cols, weights)
        gains = product(inverse, cross_rows)
        column_panel = column_panel - product(gains.T, picked_cols.T)
        return crossing - product(cross_cols, gains), row_panel, column_panel, field

    state = (crossing, row_panel, column_panel, field)
    return lax.fori_loop(0, error_var.shape[0], body, state)[3]


def shards(
    prior,
    ozone_courant,
    ozone_diffusion,
    ozone_wind,
    carbon_courant,
    carbon_diffusion,
    carbon_wind,
    ozone_sites,
    carbon_sites,
    error_var,
):
    rows, cols = prior.shape
    row_sites = ozone_sites.reshape(-1)
    col_sites = carbon_sites.reshape(-1)
    ozone = (ozone_courant, ozone_diffusion, ozone_wind)
    carbon = (carbon_courant, carbon_diffusion, carbon_wind)
    row_place = places(row_sites, rows)
    col_place = places(col_sites, cols)
    total = row_sites.size
    fits = (jnp.max(row_place[1]) < capacity(total, lax.axis_size("row"))) & (
        jnp.max(col_place[1]) < capacity(total, lax.axis_size("col"))
    )
    prepared = surroundings(
        prior, ozone, carbon, lax.axis_index("row") * rows, lax.axis_index("col") * cols
    )
    given = (prior, prepared, row_sites, col_sites, error_var, row_place, col_place)
    return lax.cond(fits, balanced, crowded, *given)


def solution(mesh):
    placed = (P("row", "col"), P(), P(), P(), P(), P(), P(), P(), P(), P())
    return jax.shard_map(
        shards, mesh=mesh, in_specs=placed, out_specs=P("row", "col"), check_vma=False
    )
```
